128 devices in a mesh: px: 8 (over y, x_lo), py: 16 (over z, x_hi, core).
Axes of the slice: x: 4 (x_hi: 2, x_lo: 2; x = x_hi * 2 + x_lo), y: 4, z: 4, core: 2. Of those that a mesh axis runs over, the one named last changes fastest.
Arguments:
- initial: float32 [256, 1024, 128], P('px', 'py'), may hold values from -6 to 6
- conduct: float32 [256, 1024, 128], P('px', 'py'), may hold values from 0.25 to 1.5
- cotangent: float32 [256, 1024, 128], P('px', 'py'), may hold values from -6 to 6
- inv_x: float32 [256, 256], replicated, may hold values from -2 to 2, as said below
- inv_y: float32 [1024, 1024], replicated, may hold values from -2 to 2, as said below
Outputs:
- adjoint: float32 [256, 1024, 128], P('px', 'py')
- gradient: float32 [256, 1024, 128], P('px', 'py')
The draws below stay inside these ranges and needn't reach their ends.
Inputs may be any that keep to these rules, and one draw needn't show every extreme that they name: `inv_x`: a dense matrix of order one. `inv_y`: a dense matrix of order one.
All inputs are finite; a program needn't handle non-finite values.
Results may differ from the reference program's by a relative error of at most 0.00013.
Values sent between devices are 32-bit elements; how exact they have to be, the bound alone decides.
A program may use at most 64 MiB of HBM per device.

```python
import math
import jax
import jax.numpy as jnp
from jax import lax

CZ = 128
STEPS = 2
NX = 256
NY = 1024


def dense_inverse(key, order):
    index = jnp.arange(order).astype(jnp.float32)
    spread = jnp.abs(index[:, None] - index[None, :])
    noise = jnp.clip(jax.random.normal(key, (order, order), jnp.float32), -4.0, 4.0)
    scale = jnp.sqrt(2.0 / order)
    return 0.8 * jnp.eye(order, dtype=jnp.float32) + noise * jnp.exp(-4.0 * spread / order) * scale


def draw_inv_x(key, part):
    return dense_inverse(jax.random.fold_in(key, 11), NX)


def draw_inv_y(key, part):
    return dense_inverse(jax.random.fold_in(key, 23), NY)


def levels(key, extent, pieces, smallest, largest):
    level, own = 1.0, jax.random.fold_in(key, 6)
    for dim, shards_of in pieces:
        heights = jnp.exp(jax.random.uniform(jax.random.fold_in(own, dim), (shards_of,), jnp.float32, smallest / len(pieces), largest / len(pieces)))
        level = level * jnp.repeat(heights, extent[dim] // shards_of).reshape([-1 if axis == dim else 1 for axis in range(len(extent))])
    return level


def centred(stream_key, dims, width, bound, shards=(), held_as=jnp.bfloat16):
    array = width * jax.random.normal(stream_key, dims, jnp.float32)
    if shards:
        array = array * levels(stream_key, dims, shards, -0.22, 0.18)
    return jnp.clip(array, -bound, bound).astype(held_as)


def setup_inputs(seed: int = 0) -> dict:
    key_of = jax.random.split(jax.random.key(seed), 6)
    return {
        "initial": centred(key_of[0], (NX, NY, CZ), 1.0, 6.0, ((0, 8), (1, 16)), jnp.float32),
        "conduct": jnp.clip(jnp.exp(math.log(1.5) - 1.7917595 * jax.random.uniform(key_of[1], (NX, NY, CZ), jnp.float32) ** levels(key_of[1], (NX, NY, CZ), ((0, 8), (1, 16)), -0.2, 0.2)), 0.25, 1.5),
        "cotangent": centred(key_of[2], (NX, NY, CZ), 1.0, 6.0, ((0, 8), (1, 16)), jnp.float32),
        "inv_x": draw_inv_x(jax.random.fold_in(key_of[5], 71), 0),
        "inv_y": draw_inv_y(jax.random.fold_in(key_of[5], 71), 0),
    }


RATE = 0.2

def xdiff(field):
    padded = jnp.pad(field, ((1, 1), (0, 0), (0, 0)))
    return padded[2:] + padded[:-2] - 2.0 * field

def ydiff(field):
    padded = jnp.pad(field, ((0, 0), (1, 1), (0, 0)))
    return padded[:, 2:] + padded[:, :-2] - 2.0 * field

def zoperate(field, conduct):
    upper = jnp.concatenate([field[:, :, 1:], jnp.zeros_like(field[:, :, :1])], axis=2)
    flux = conduct * (upper - field)
    lower = jnp.concatenate([jnp.zeros_like(flux[:, :, :1]), flux[:, :, :-1]], axis=2)
    return flux - lower

def forward(initial, conduct, inv_x, inv_y):
    state = initial
    for step in range(STEPS):
        first = state + RATE * (ydiff(state) + zoperate(state, conduct))
        half = jnp.einsum('ij,jyz->iyz', inv_x, first, precision=lax.Precision.HIGHEST)
        second = half + RATE * (xdiff(half) + zoperate(half, conduct))
        state = jnp.einsum('ij,xjz->xiz', inv_y, second, precision=lax.Precision.HIGHEST)
    return state

def reference(initial, conduct, cotangent, inv_x, inv_y):
    result, pullback = jax.vjp(lambda first, second: forward(first, second, inv_x, inv_y), initial, conduct)
    adjoint, gradient = pullback(cotangent)
    return (adjoint, gradient)
```

```python
import jax
import jax.numpy as jnp
from jax import lax
from jax.sharding import PartitionSpec as P

RATE = 0.2
LINES = ("py", "px")


def ydiff_block(field):
    count = lax.axis_size("py")
    head = field[:, :1]
    tail = field[:, -1:]
    below = lax.ppermute(tail, "py", [(i, i + 1) for i in range(count - 1)])
    above = lax.ppermute(head, "py", [(i + 1, i) for i in range(count - 1)])
    padded = jnp.concatenate([below, field, above], axis=1)
    return padded[:, 2:] + padded[:, :-2] - 2.0 * field


def diff_along(field, dim):
    pad = [(0, 0)] * field.ndim
    pad[dim] = (1, 1)
    padded = jnp.pad(field, pad)
    n = field.shape[dim]
    return (
        lax.slice_in_dim(padded, 2, n + 2, axis=dim)
        + lax.slice_in_dim(padded, 0, n, axis=dim)
        - 2.0 * field
    )


def zoperate(field, conduct):
    upper = jnp.concatenate([field[:, :, 1:], jnp.zeros_like(field[:, :, :1])], axis=2)
    flux = conduct * (upper - field)
    lower = jnp.concatenate([jnp.zeros_like(flux[:, :, :1]), flux[:, :, :-1]], axis=2)
    return flux - lower


def zstep(field):
    upper = jnp.concatenate([field[:, :, 1:], jnp.zeros_like(field[:, :, :1])], axis=2)
    return upper - field


def apply(matrix, field, form):
    return jnp.einsum(form, matrix, field, precision=lax.Precision.HIGHEST)


def block_to_x(stack):
    return lax.all_to_all(stack, "px", split_axis=2, concat_axis=1, tiled=True)


def x_to_block(stack):
    return lax.all_to_all(stack, "px", split_axis=1, concat_axis=2, tiled=True)


def x_to_y(stack):
    return lax.all_to_all(stack, LINES, split_axis=1, concat_axis=2, tiled=True)


def y_to_x(stack):
    return lax.all_to_all(stack, LINES, split_axis=2, concat_axis=1, tiled=True)


def local(initial, conduct, cotangent, inv_x, inv_y):
    first0 = initial + RATE * (ydiff_block(initial) + zoperate(initial, conduct))
    f0x, cx, tx = block_to_x(jnp.stack([first0, conduct, cotangent]))
    half0 = apply(inv_x, f0x, "ij,jyz->iyz")
    second0 = half0 + RATE * (diff_along(half0, 0) + zoperate(half0, cx))
    s0y, cy, ty = x_to_y(jnp.stack([second0, cx, tx]))
    state1 = apply(inv_y, s0y, "ij,xjz->xiz")
    first1 = state1 + RATE * (diff_along(state1, 1) + zoperate(state1, cy))
    lam_second1 = apply(inv_y, ty, "ji,xjz->xiz")
    f1x, ls1x = y_to_x(jnp.stack([first1, lam_second1]))
    half1 = apply(inv_x, f1x, "ij,jyz->iyz")
    grad_x = -RATE * zstep(ls1x) * zstep(half1)
    lam_half1 = ls1x + RATE * (diff_along(ls1x, 0) + zoperate(ls1x, cx))
    lam_first1 = apply(inv_x, lam_half1, "ji,jyz->iyz")
    (lf1y,) = x_to_y(lam_first1[None])
    grad_y = -RATE * zstep(lf1y) * zstep(state1)
    lam_state1 = lf1y + RATE * (diff_along(lf1y, 1) + zoperate(lf1y, cy))
    lam_second0 = apply(inv_y, lam_state1, "ji,xjz->xiz")
    ls0x, gyx = y_to_x(jnp.stack([lam_second0, grad_y]))
    grad_x = grad_x + gyx - RATE * zstep(ls0x) * zstep(half0)
    lam_half0 = ls0x + RATE * (diff_along(ls0x, 0) + zoperate(ls0x, cx))
    lam_first0 = apply(inv_x, lam_half0, "ji,jyz->iyz")
    lf0, gb = x_to_block(jnp.stack([lam_first0, grad_x]))
    gradient = gb - RATE * zstep(lf0) * zstep(initial)
    adjoint = lf0 + RATE * (ydiff_block(lf0) + zoperate(lf0, conduct))
    return (adjoint, gradient)


def solution(mesh):
    in_specs = (P("px", "py", None), P("px", "py", None), P("px", "py", None), P(), P())
    out_specs = (P("px", "py", None), P("px", "py", None))
    return jax.shard_map(local, mesh=mesh, in_specs=in_specs, out_specs=out_specs, check_vma=False)
```

```python
import jax
import jax.numpy as jnp
from jax import lax
from jax.sharding import PartitionSpec as P

RATE = 0.2
LINES = ("py", "px")
HIGH = lax.Precision.HIGHEST


def ydiff_block(field):
    count = lax.axis_size("py")
    below = lax.ppermute(field[:, -1:], "py", [(i, i + 1) for i in range(count - 1)])
    above = lax.ppermute(field[:, :1], "py", [(i + 1, i) for i in range(count - 1)])
    padded = jnp.concatenate([below, field, above], axis=1)
    return padded[:, 2:] + padded[:, :-2] - 2.0 * field


def zoperate_block(field, conduct):
    upper = jnp.concatenate([field[:, :, 1:], jnp.zeros_like(field[:, :, :1])], axis=2)
    flux = conduct * (upper - field)
    lower = jnp.concatenate([jnp.zeros_like(flux[:, :, :1]), flux[:, :, :-1]], axis=2)
    return flux - lower


def zstep_block(field):
    upper = jnp.concatenate([field[:, :, 1:], jnp.zeros_like(field[:, :, :1])], axis=2)
    return upper - field


def zstep(field):
    upper = jnp.concatenate([field[1:], jnp.zeros_like(field[:1])], axis=0)
    return upper - field


def zoperate(field, conduct):
    flux = conduct * zstep(field)
    lower = jnp.concatenate([jnp.zeros_like(flux[:1]), flux[:-1]], axis=0)
    return flux - lower


def xdiff(field):
    padded = jnp.pad(field, ((0, 0), (0, 0), (1, 1)))
    return padded[:, :, 2:] + padded[:, :, :-2] - 2.0 * field


def mesh_index(line):
    rows = lax.axis_size("px")
    cols = lax.axis_size("py")
    return (line % rows) * cols + line // rows


def ydiff(field):
    count = lax.axis_size(LINES)
    up = [(mesh_index(i), mesh_index(i + 1)) for i in range(count - 1)]
    down = [(b, a) for a, b in up]
    below = lax.ppermute(field[:, -1:], ("px", "py"), up)
    above = lax.ppermute(field[:, :1], ("px", "py"), down)
    padded = jnp.concatenate([below, field, above], axis=1)
    return padded[:, 2:] + padded[:, :-2] - 2.0 * field


def along_x(field, matrix, transpose):
    dims = (((2,), (0,)), ((), ())) if transpose else (((2,), (1,)), ((), ()))
    return lax.dot_general(field, matrix, dims, precision=HIGH)


def along_y(matrix, field, transpose):
    dims = (((0,), (0,)), ((), ())) if transpose else (((1,), (0,)), ((), ()))
    return lax.dot_general(matrix, field, dims, precision=HIGH)


def block_to_x(*fields):
    joined = jnp.concatenate(fields, axis=2)
    lines = lax.all_to_all(joined, "px", split_axis=1, concat_axis=0, tiled=True)
    depth = fields[0].shape[2]
    return [jnp.transpose(lines[:, :, k * depth:(k + 1) * depth], (2, 1, 0)) for k in range(len(fields))]


def x_to_block(*fields):
    joined = jnp.concatenate([jnp.transpose(f, (2, 1, 0)) for f in fields], axis=2)
    block = lax.all_to_all(joined, "px", split_axis=0, concat_axis=1, tiled=True)
    depth = fields[0].shape[0]
    return [block[:, :, k * depth:(k + 1) * depth] for k in range(len(fields))]


def x_to_y(*fields):
    joined = jnp.concatenate(fields, axis=2)
    lines = lax.all_to_all(joined, LINES, split_axis=0, concat_axis=1, tiled=True)[0]
    width = fields[0].shape[2]
    return [lines[:, k * width:(k + 1) * width] for k in range(len(fields))]


def y_to_x(*fields):
    joined = jnp.concatenate(fields, axis=1)[None]
    lines = lax.all_to_all(joined, LINES, split_axis=1, concat_axis=0, tiled=True)
    width = fields[0].shape[1]
    return [lines[:, :, k * width:(k + 1) * width] for k in range(len(fields))]


def local(initial, conduct, cotangent, inv_x, inv_y):
    first0 = initial + RATE * (ydiff_block(initial) + zoperate_block(initial, conduct))
    f0x, cx, tx = block_to_x(first0, conduct, cotangent)
    half0 = along_x(f0x, inv_x, False)
    second0 = half0 + RATE * (xdiff(half0) + zoperate(half0, cx))
    s0y, ty = x_to_y(second0, tx)
    state1_y = along_y(inv_y, s0y, False)
    lam_second1_y = along_y(inv_y, ty, True)
    state1, ls1 = y_to_x(state1_y, lam_second1_y)
    first1 = state1 + RATE * (ydiff(state1) + zoperate(state1, cx))
    half1 = along_x(first1, inv_x, False)
    grad = -RATE * zstep(ls1) * zstep(half1)
    lam_half1 = ls1 + RATE * (xdiff(ls1) + zoperate(ls1, cx))
    lam_first1 = along_x(lam_half1, inv_x, True)
    grad = grad - RATE * zstep(lam_first1) * zstep(state1)
    lam_state1 = lam_first1 + RATE * (ydiff(lam_first1) + zoperate(lam_first1, cx))
    (lsy,) = x_to_y(lam_state1)
    lam_second0_y = along_y(inv_y, lsy, True)
    (ls0,) = y_to_x(lam_second0_y)
    grad = grad - RATE * zstep(ls0) * zstep(half0)
    lam_half0 = ls0 + RATE * (xdiff(ls0) + zoperate(ls0, cx))
    lam_first0 = along_x(lam_half0, inv_x, True)
    lf0, gb = x_to_block(lam_first0, grad)
    gradient = gb - RATE * zstep_block(lf0) * zstep_block(initial)
    adjoint = lf0 + RATE * (ydiff_block(lf0) + zoperate_block(lf0, conduct))
    return (adjoint, gradient)


def solution(mesh):
    in_specs = (P("px", "py", None), P("px", "py", None), P("px", "py", None), P(), P())
    out_specs = (P("px", "py", None), P("px", "py", None))
    return jax.shard_map(local, mesh=mesh, in_specs=in_specs, out_specs=out_specs, check_vma=False)
```

```python
import jax
import jax.numpy as jnp
from jax import lax
from jax.sharding import PartitionSpec as P

RATE = 0.2
LINES = ("py", "px")
HIGH = lax.Precision.HIGHEST


def ydiff_block(field):
    count = lax.axis_size("py")
    below = lax.ppermute(field[:, -1:], "py", [(i, i + 1) for i in range(count - 1)])
    above = lax.ppermute(field[:, :1], "py", [(i + 1, i) for i in range(count - 1)])
    padded = jnp.concatenate([below, field, above], axis=1)
    return padded[:, 2:] + padded[:, :-2] - 2.0 * field


def zoperate_block(field, conduct):
    upper = jnp.concatenate([field[:, :, 1:], jnp.zeros_like(field[:, :, :1])], axis=2)
    flux = conduct * (upper - field)
    lower = jnp.concatenate([jnp.zeros_like(flux[:, :, :1]), flux[:, :, :-1]], axis=2)
    return flux - lower


def zstep_block(field):
    upper = jnp.concatenate([field[:, :, 1:], jnp.zeros_like(field[:, :, :1])], axis=2)
    return upper - field


def zstep(field):
    upper = jnp.concatenate([field[1:], jnp.zeros_like(field[:1])], axis=0)
    return upper - field


def zoperate(field, conduct):
    flux = conduct * zstep(field)
    lower = jnp.concatenate([jnp.zeros_like(flux[:1]), flux[:-1]], axis=0)
    return flux - lower


def xdiff(field):
    padded = jnp.pad(field, ((0, 0), (0, 0), (1, 1)))
    return padded[:, :, 2:] + padded[:, :, :-2] - 2.0 * field


def mesh_index(line):
    rows = lax.axis_size("px")
    cols = lax.axis_size("py")
    return (line % rows) * cols + line // rows


def ydiff(field):
    count = lax.axis_size(LINES)
    up = [(mesh_index(i), mesh_index(i + 1)) for i in range(count - 1)]
    down = [(b, a) for a, b in up]
    below = lax.ppermute(field[:, -1:], ("px", "py"), up)
    above = lax.ppermute(field[:, :1], ("px", "py"), down)
    padded = jnp.concatenate([below, field, above], axis=1)
    return padded[:, 2:] + padded[:, :-2] - 2.0 * field


def along_x(field, matrix, transpose):
    dims = (((2,), (0,)), ((), ())) if transpose else (((2,), (1,)), ((), ()))
    return lax.dot_general(field, matrix, dims, precision=HIGH)


def along_y(matrix, field, transpose):
    dims = (((0,), (0,)), ((), ())) if transpose else (((1,), (0,)), ((), ()))
    return lax.dot_general(matrix, field, dims, precision=HIGH)


def block_to_x(*fields):
    joined = jnp.concatenate(fields, axis=2)
    lines = lax.all_to_all(joined, "px", split_axis=1, concat_axis=0, tiled=True)
    depth = fields[0].shape[2]
    return [jnp.transpose(lines[:, :, k * depth:(k + 1) * depth], (2, 1, 0)) for k in range(len(fields))]


def x_to_block(*fields):
    joined = jnp.concatenate([jnp.transpose(f, (2, 1, 0)) for f in fields], axis=2)
    block = lax.all_to_all(joined, "px", split_axis=0, concat_axis=1, tiled=True)
    depth = fields[0].shape[0]
    return [block[:, :, k * depth:(k + 1) * depth] for k in range(len(fields))]


def x_to_y(*fields):
    joined = jnp.concatenate(fields, axis=2)
    lines = lax.all_to_all(joined, LINES, split_axis=0, concat_axis=0, tiled=True)
    lines = lines.reshape(-1, lines.shape[2])
    width = fields[0].shape[2]
    return [lines[:, k * width:(k + 1) * width] for k in range(len(fields))]


def y_to_x(*fields):
    joined = jnp.concatenate(fields, axis=1)
    count = lax.axis_size(LINES)
    joined = joined.reshape(count, -1, joined.shape[1])
    lines = lax.all_to_all(joined, LINES, split_axis=0, concat_axis=0, tiled=True)
    width = fields[0].shape[1]
    return [lines[:, :, k * width:(k + 1) * width] for k in range(len(fields))]


def local(initial, conduct, cotangent, inv_x, inv_y):
    first0 = initial + RATE * (ydiff_block(initial) + zoperate_block(initial, conduct))
    f0x, cx, tx = block_to_x(first0, conduct, cotangent)
    half0 = along_x(f0x, inv_x, False)
    second0 = half0 + RATE * (xdiff(half0) + zoperate(half0, cx))
    s0y, ty = x_to_y(second0, tx)
    state1_y = along_y(inv_y, s0y, False)
    lam_second1_y = along_y(inv_y, ty, True)
    state1, ls1 = y_to_x(state1_y, lam_second1_y)
    first1 = state1 + RATE * (ydiff(state1) + zoperate(state1, cx))
    half1 = along_x(first1, inv_x, False)
    grad = -RATE * zstep(ls1) * zstep(half1)
    lam_half1 = ls1 + RATE * (xdiff(ls1) + zoperate(ls1, cx))
    lam_first1 = along_x(lam_half1, inv_x, True)
    grad = grad - RATE * zstep(lam_first1) * zstep(state1)
    lam_state1 = lam_first1 + RATE * (ydiff(lam_first1) + zoperate(lam_first1, cx))
    (lsy,) = x_to_y(lam_state1)
    lam_second0_y = along_y(inv_y, lsy, True)
    (ls0,) = y_to_x(lam_second0_y)
    grad = grad - RATE * zstep(ls0) * zstep(half0)
    lam_half0 = ls0 + RATE * (xdiff(ls0) + zoperate(ls0, cx))
    lam_first0 = along_x(lam_half0, inv_x, True)
    lf0, gb = x_to_block(lam_first0, grad)
    gradient = gb - RATE * zstep_block(lf0) * zstep_block(initial)
    adjoint = lf0 + RATE * (ydiff_block(lf0) + zoperate_block(lf0, conduct))
    return (adjoint, gradient)


def solution(mesh):
    in_specs = (P("px", "py", None), P("px", "py", None), P("px", "py", None), P(), P())
    out_specs = (P("px", "py", None), P("px", "py", None))
    return jax.shard_map(local, mesh=mesh, in_specs=in_specs, out_specs=out_specs, check_vma=False)
```

```python
import jax
import jax.numpy as jnp
from jax import lax
from jax.sharding import PartitionSpec as P

RATE = 0.2
LINES = ("py", "px")
HIGH = lax.Precision.HIGHEST


def ydiff_block(field):
    count = lax.axis_size("py")
    below = lax.ppermute(field[:, -1:], "py", [(i, i + 1) for i in range(count - 1)])
    above = lax.ppermute(field[:, :1], "py", [(i + 1, i) for i in range(count - 1)])
    padded = jnp.concatenate([below, field, above], axis=1)
    return padded[:, 2:] + padded[:, :-2] - 2.0 * field


def zoperate_block(field, conduct):
    upper = jnp.concatenate([field[:, :, 1:], jnp.zeros_like(field[:, :, :1])], axis=2)
    flux = conduct * (upper - field)
    lower = jnp.concatenate([jnp.zeros_like(flux[:, :, :1]), flux[:, :, :-1]], axis=2)
    return flux - lower


def zstep_block(field):
    upper = jnp.concatenate([field[:, :, 1:], jnp.zeros_like(field[:, :, :1])], axis=2)
    return upper - field


def zstep(field):
    upper = jnp.concatenate([field[1:], jnp.zeros_like(field[:1])], axis=0)
    return upper - field


def zoperate(field, conduct):
    flux = conduct * zstep(field)
    lower = jnp.concatenate([jnp.zeros_like(flux[:1]), flux[:-1]], axis=0)
    return flux - lower


def xdiff(field):
    padded = jnp.pad(field, ((0, 0), (0, 0), (1, 1)))
    return padded[:, :, 2:] + padded[:, :, :-2] - 2.0 * field


def mesh_index(line):
    rows = lax.axis_size("px")
    cols = lax.axis_size("py")
    return (line % rows) * cols + line // rows


def along_x(field, matrix, transpose):
    dims = (((2,), (0,)), ((), ())) if transpose else (((2,), (1,)), ((), ()))
    return lax.dot_general(field, matrix, dims, precision=HIGH)


def along_y(matrix, field, transpose):
    dims = (((0,), (0,)), ((), ())) if transpose else (((1,), (0,)), ((), ()))
    return lax.dot_general(matrix, field, dims, precision=HIGH)


def block_to_x(*fields):
    joined = jnp.concatenate(fields, axis=2)
    lines = lax.all_to_all(joined, "px", split_axis=1, concat_axis=0, tiled=True)
    depth = fields[0].shape[2]
    return [jnp.transpose(lines[:, :, k * depth:(k + 1) * depth], (2, 1, 0)) for k in range(len(fields))]


def x_to_block(*fields):
    joined = jnp.concatenate([jnp.transpose(f, (2, 1, 0)) for f in fields], axis=2)
    block = lax.all_to_all(joined, "px", split_axis=0, concat_axis=1, tiled=True)
    depth = fields[0].shape[0]
    return [block[:, :, k * depth:(k + 1) * depth] for k in range(len(fields))]


def x_to_y(*fields):
    joined = jnp.concatenate(fields, axis=2)
    lines = lax.all_to_all(joined, LINES, split_axis=0, concat_axis=0, tiled=True)
    lines = lines.reshape(-1, lines.shape[2])
    width = fields[0].shape[2]
    return [lines[:, k * width:(k + 1) * width] for k in range(len(fields))]


def y_to_x(*fields):
    joined = jnp.concatenate(fields, axis=1)
    count = lax.axis_size(LINES)
    joined = joined.reshape(count, -1, joined.shape[1])
    lines = lax.all_to_all(joined, LINES, split_axis=0, concat_axis=0, tiled=True)
    width = fields[0].shape[1]
    return [lines[:, :, k * width:(k + 1) * width] for k in range(len(fields))]


def y_to_x_wide(*fields):
    count = lax.axis_size(LINES)
    wides = []
    for field in fields:
        blocks = field.reshape(count, -1, field.shape[1])
        zero = jnp.zeros_like(blocks[:1, :1])
        below = jnp.concatenate([zero, blocks[:-1, -1:]], axis=0)
        above = jnp.concatenate([blocks[1:, :1], zero], axis=0)
        wides.append(jnp.concatenate([below, blocks, above], axis=1))
    joined = jnp.concatenate(wides, axis=2)
    lines = lax.all_to_all(joined, LINES, split_axis=0, concat_axis=0, tiled=True)
    width = fields[0].shape[1]
    return [lines[:, :, k * width:(k + 1) * width] for k in range(len(fields))]


def widen(field):
    count = lax.axis_size(LINES)
    up = [(mesh_index(i), mesh_index(i + 1)) for i in range(count - 1)]
    down = [(b, a) for a, b in up]
    below = lax.ppermute(field[:, -1:], ("px", "py"), up)
    above = lax.ppermute(field[:, :1], ("px", "py"), down)
    return jnp.concatenate([below, field, above], axis=1)


def ydiff_wide(wide):
    return wide[:, 2:] + wide[:, :-2] - 2.0 * wide[:, 1:-1]


def local(initial, conduct, cotangent, inv_x, inv_y):
    first0 = initial + RATE * (ydiff_block(initial) + zoperate_block(initial, conduct))
    f0x, cx, tx = block_to_x(first0, conduct, cotangent)
    half0 = along_x(f0x, inv_x, False)
    second0 = half0 + RATE * (xdiff(half0) + zoperate(half0, cx))
    s0y, ty = x_to_y(second0, tx)
    state1_y = along_y(inv_y, s0y, False)
    lam_second1_y = along_y(inv_y, ty, True)
    state1w, ls1w = y_to_x_wide(state1_y, lam_second1_y)
    cxw = widen(cx)
    state1 = state1w[:, 1:-1]
    ls1 = ls1w[:, 1:-1]
    first1 = state1 + RATE * (ydiff_wide(state1w) + zoperate(state1, cx))
    half1 = along_x(first1, inv_x, False)
    grad = -RATE * zstep(ls1) * zstep(half1)
    lam_half1w = ls1w + RATE * (xdiff(ls1w) + zoperate(ls1w, cxw))
    lam_first1w = along_x(lam_half1w, inv_x, True)
    lam_first1 = lam_first1w[:, 1:-1]
    grad = grad - RATE * zstep(lam_first1) * zstep(state1)
    lam_state1 = lam_first1 + RATE * (ydiff_wide(lam_first1w) + zoperate(lam_first1, cx))
    (lsy,) = x_to_y(lam_state1)
    lam_second0_y = along_y(inv_y, lsy, True)
    (ls0,) = y_to_x(lam_second0_y)
    grad = grad - RATE * zstep(ls0) * zstep(half0)
    lam_half0 = ls0 + RATE * (xdiff(ls0) + zoperate(ls0, cx))
    lam_first0 = along_x(lam_half0, inv_x, True)
    lf0, gb = x_to_block(lam_first0, grad)
    gradient = gb - RATE * zstep_block(lf0) * zstep_block(initial)
    adjoint = lf0 + RATE * (ydiff_block(lf0) + zoperate_block(lf0, conduct))
    return (adjoint, gradient)


def solution(mesh):
    in_specs = (P("px", "py", None), P("px", "py", None), P("px", "py", None), P(), P())
    out_specs = (P("px", "py", None), P("px", "py", None))
    return jax.shard_map(local, mesh=mesh, in_specs=in_specs, out_specs=out_specs, check_vma=False)
```

```python
import jax
import jax.numpy as jnp
from jax import lax
from jax.sharding import PartitionSpec as P

RATE = 0.2
LINES = ("py", "px")
HIGH = lax.Precision.HIGHEST


def ydiff_block(field):
    count = lax.axis_size("py")
    below = lax.ppermute(field[:, -1:], "py", [(i, i + 1) for i in range(count - 1)])
    above = lax.ppermute(field[:, :1], "py", [(i + 1, i) for i in range(count - 1)])
    padded = jnp.concatenate([below, field, above], axis=1)
    return padded[:, 2:] + padded[:, :-2] - 2.0 * field


def zoperate_block(field, conduct):
    upper = jnp.concatenate([field[:, :, 1:], jnp.zeros_like(field[:, :, :1])], axis=2)
    flux = conduct * (upper - field)
    lower = jnp.concatenate([jnp.zeros_like(flux[:, :, :1]), flux[:, :, :-1]], axis=2)
    return flux - lower


def zstep_block(field):
    upper = jnp.concatenate([field[:, :, 1:], jnp.zeros_like(field[:, :, :1])], axis=2)
    return upper - field


def zstep(field):
    upper = jnp.concatenate([field[1:], jnp.zeros_like(field[:1])], axis=0)
    return upper - field


def zoperate(field, conduct):
    flux = conduct * zstep(field)
    lower = jnp.concatenate([jnp.zeros_like(flux[:1]), flux[:-1]], axis=0)
    return flux - lower


def xdiff(field):
    padded = jnp.pad(field, ((0, 0), (0, 0), (1, 1)))
    return padded[:, :, 2:] + padded[:, :, :-2] - 2.0 * field


def mesh_index(line):
    rows = lax.axis_size("px")
    cols = lax.axis_size("py")
    return (line % rows) * cols + line // rows


def along_x(field, matrix, transpose):
    dims = (((2,), (0,)), ((), ())) if transpose else (((2,), (1,)), ((), ()))
    return lax.dot_general(field, matrix, dims, precision=HIGH)


def along_y(matrix, field, transpose):
    dims = (((0,), (0,)), ((), ())) if transpose else (((1,), (0,)), ((), ()))
    return lax.dot_general(matrix, field, dims, precision=HIGH)


def block_to_x(*fields):
    joined = jnp.concatenate(fields, axis=2)
    lines = lax.all_to_all(joined, "px", split_axis=1, concat_axis=0, tiled=True)
    depth = fields[0].shape[2]
    return [jnp.transpose(lines[:, :, k * depth:(k + 1) * depth], (2, 1, 0)) for k in range(len(fields))]


def x_to_block(*fields):
    joined = jnp.concatenate([jnp.transpose(f, (2, 1, 0)) for f in fields], axis=2)
    block = lax.all_to_all(joined, "px", split_axis=0, concat_axis=1, tiled=True)
    depth = fields[0].shape[0]
    return [block[:, :, k * depth:(k + 1) * depth] for k in range(len(fields))]


def x_to_y(*fields):
    joined = jnp.concatenate(fields, axis=2)
    lines = lax.all_to_all(joined, LINES, split_axis=0, concat_axis=0, tiled=True)
    lines = lines.reshape(-1, lines.shape[2])
    width = fields[0].shape[2]
    return [lines[:, k * width:(k + 1) * width] for k in range(len(fields))]


def y_to_x(*fields):
    joined = jnp.concatenate(fields, axis=1)
    count = lax.axis_size(LINES)
    joined = joined.reshape(count, -1, joined.shape[1])
    lines = lax.all_to_all(joined, LINES, split_axis=0, concat_axis=0, tiled=True)
    width = fields[0].shape[1]
    return [lines[:, :, k * width:(k + 1) * width] for k in range(len(fields))]


def y_to_x_wide(*fields):
    count = lax.axis_size(LINES)
    width = fields[0].shape[1]
    blocks = [f.reshape(count, -1, width) for f in fields]
    edges = []
    for block in blocks:
        zero = jnp.zeros_like(block[:1, :1])
        edges.append(jnp.concatenate([zero, block[:-1, -1:]], axis=0))
        edges.append(jnp.concatenate([block[1:, :1], zero], axis=0))
    rows = blocks[0].shape[1]
    packed = jnp.concatenate(edges, axis=1).reshape(count, rows, -1)
    joined = jnp.concatenate(blocks + [packed], axis=2)
    lines = lax.all_to_all(joined, LINES, split_axis=0, concat_axis=0, tiled=True)
    depth = lines.shape[0]
    edge = lines[:, :, len(fields) * width:].reshape(depth, 2 * len(fields), width)
    wides = []
    for k in range(len(fields)):
        core = lines[:, :, k * width:(k + 1) * width]
        wides.append(jnp.concatenate([edge[:, 2 * k:2 * k + 1], core, edge[:, 2 * k + 1:2 * k + 2]], axis=1))
    return wides


def widen(field):
    count = lax.axis_size(LINES)
    up = [(mesh_index(i), mesh_index(i + 1)) for i in range(count - 1)]
    down = [(b, a) for a, b in up]
    below = lax.ppermute(field[:, -1:], ("px", "py"), up)
    above = lax.ppermute(field[:, :1], ("px", "py"), down)
    return jnp.concatenate([below, field, above], axis=1)


def ydiff_wide(wide):
    return wide[:, 2:] + wide[:, :-2] - 2.0 * wide[:, 1:-1]


def local(initial, conduct, cotangent, inv_x, inv_y):
    first0 = initial + RATE * (ydiff_block(initial) + zoperate_block(initial, conduct))
    f0x, cx, tx = block_to_x(first0, conduct, cotangent)
    half0 = along_x(f0x, inv_x, False)
    second0 = half0 + RATE * (xdiff(half0) + zoperate(half0, cx))
    s0y, ty = x_to_y(second0, tx)
    state1_y = along_y(inv_y, s0y, False)
    lam_second1_y = along_y(inv_y, ty, True)
    state1w, ls1w = y_to_x_wide(state1_y, lam_second1_y)
    cxw = widen(cx)
    state1 = state1w[:, 1:-1]
    ls1 = ls1w[:, 1:-1]
    first1 = state1 + RATE * (ydiff_wide(state1w) + zoperate(state1, cx))
    half1 = along_x(first1, inv_x, False)
    grad = -RATE * zstep(ls1) * zstep(half1)
    lam_half1w = ls1w + RATE * (xdiff(ls1w) + zoperate(ls1w, cxw))
    lam_first1w = along_x(lam_half1w, inv_x, True)
    lam_first1 = lam_first1w[:, 1:-1]
    grad = grad - RATE * zstep(lam_first1) * zstep(state1)
    lam_state1 = lam_first1 + RATE * (ydiff_wide(lam_first1w) + zoperate(lam_first1, cx))
    (lsy,) = x_to_y(lam_state1)
    lam_second0_y = along_y(inv_y, lsy, True)
    (ls0,) = y_to_x(lam_second0_y)
    grad = grad - RATE * zstep(ls0) * zstep(half0)
    lam_half0 = ls0 + RATE * (xdiff(ls0) + zoperate(ls0, cx))
    lam_first0 = along_x(lam_half0, inv_x, True)
    lf0, gb = x_to_block(lam_first0, grad)
    gradient = gb - RATE * zstep_block(lf0) * zstep_block(initial)
    adjoint = lf0 + RATE * (ydiff_block(lf0) + zoperate_block(lf0, conduct))
    return (adjoint, gradient)


def solution(mesh):
    in_specs = (P("px", "py", None), P("px", "py", None), P("px", "py", None), P(), P())
    out_specs = (P("px", "py", None), P("px", "py", None))
    return jax.shard_map(local, mesh=mesh, in_specs=in_specs, out_specs=out_specs, check_vma=False)
```

```python
import functools

import jax
import jax.numpy as jnp
from jax import lax
from jax.experimental import pallas as pl
from jax.experimental.pallas import tpu as pltpu
from jax.sharding import PartitionSpec as P

RATE = 0.2
LINES = ("py", "px")
HIGH = lax.Precision.HIGHEST


def _neighbours(lines):
    rows = lax.axis_size("px")
    if lines:
        me = lax.axis_index("py") * rows + lax.axis_index("px")
        count = rows * lax.axis_size("py")

        def device(k):
            return (lax.rem(k, rows), lax.div(k, rows))
    else:
        me = lax.axis_index("py")
        count = lax.axis_size("py")

        def device(k):
            return (lax.axis_index("px"), k)
    return me, count, device


def _halo_kernel(lines, x_ref, o_ref, low, high, sems):
    me, count, device = _neighbours(lines)
    has_low = me > 0
    has_high = me < count - 1
    mesh = pl.DeviceIdType.MESH
    barrier = pltpu.get_barrier_semaphore()

    @pl.when(has_low)
    def _():
        pl.semaphore_signal(barrier, inc=1, device_id=device(me - 1), device_id_type=mesh)

    @pl.when(has_high)
    def _():
        pl.semaphore_signal(barrier, inc=1, device_id=device(me + 1), device_id_type=mesh)

    pl.semaphore_wait(barrier, has_low.astype(jnp.int32) + has_high.astype(jnp.int32))
    rows = x_ref.shape[1]

    def up():
        return pltpu.make_async_remote_copy(
            src_ref=x_ref.at[:, pl.ds(rows - 1, 1)], dst_ref=low, send_sem=sems.at[0],
            recv_sem=sems.at[1], device_id=device(me + 1), device_id_type=mesh)

    def down():
        return pltpu.make_async_remote_copy(
            src_ref=x_ref.at[:, pl.ds(0, 1)], dst_ref=high, send_sem=sems.at[2],
            recv_sem=sems.at[3], device_id=device(me - 1), device_id_type=mesh)

    @pl.when(has_high)
    def _():
        up().start()

    @pl.when(has_low)
    def _():
        down().start()

    @pl.when(jnp.logical_not(has_low))
    def _():
        low[...] = jnp.zeros_like(low)

    @pl.when(jnp.logical_not(has_high))
    def _():
        high[...] = jnp.zeros_like(high)

    field = x_ref[...]
    o_ref[:, 1:rows - 1] = field[:, 2:] + field[:, :-2] - 2.0 * field[:, 1:-1]

    @pl.when(has_high)
    def _():
        up().wait_send()
        down_recv = pltpu.make_async_remote_copy(
            src_ref=x_ref.at[:, pl.ds(0, 1)], dst_ref=high, send_sem=sems.at[2],
            recv_sem=sems.at[3], device_id=device(me + 1), device_id_type=mesh)
        down_recv.wait_recv()

    @pl.when(has_low)
    def _():
        down().wait_send()
        up_recv = pltpu.make_async_remote_copy(
            src_ref=x_ref.at[:, pl.ds(rows - 1, 1)], dst_ref=low, send_sem=sems.at[0],
            recv_sem=sems.at[1], device_id=device(me - 1), device_id_type=mesh)
        up_recv.wait_recv()

    o_ref[:, 0:1] = field[:, 1:2] + low[...] - 2.0 * field[:, 0:1]
    o_ref[:, rows - 1:rows] = high[...] + field[:, rows - 2:rows - 1] - 2.0 * field[:, rows - 1:rows]


_HALO_IDS = {}


def halo_diff(field, lines):
    key = (lines, field.shape)
    cid = _HALO_IDS.setdefault(key, len(_HALO_IDS))
    edge = (field.shape[0], 1, field.shape[2])
    return pl.pallas_call(
        functools.partial(_halo_kernel, lines),
        out_shape=jax.ShapeDtypeStruct(field.shape, field.dtype),
        in_specs=[pl.BlockSpec(memory_space=pltpu.VMEM)],
        out_specs=pl.BlockSpec(memory_space=pltpu.VMEM),
        scratch_shapes=[
            pltpu.VMEM(edge, field.dtype),
            pltpu.VMEM(edge, field.dtype),
            pltpu.SemaphoreType.DMA((4,)),
        ],
        compiler_params=pltpu.CompilerParams(collective_id=cid, has_side_effects=True),
    )(field)


def zoperate_block(field, conduct):
    upper = jnp.concatenate([field[:, :, 1:], jnp.zeros_like(field[:, :, :1])], axis=2)
    flux = conduct * (upper - field)
    lower = jnp.concatenate([jnp.zeros_like(flux[:, :, :1]), flux[:, :, :-1]], axis=2)
    return flux - lower


def zstep_block(field):
    upper = jnp.concatenate([field[:, :, 1:], jnp.zeros_like(field[:, :, :1])], axis=2)
    return upper - field


def zstep(field):
    upper = jnp.concatenate([field[1:], jnp.zeros_like(field[:1])], axis=0)
    return upper - field


def zoperate(field, conduct):
    flux = conduct * zstep(field)
    lower = jnp.concatenate([jnp.zeros_like(flux[:1]), flux[:-1]], axis=0)
    return flux - lower


def xdiff(field):
    padded = jnp.pad(field, ((0, 0), (0, 0), (1, 1)))
    return padded[:, :, 2:] + padded[:, :, :-2] - 2.0 * field


def along_x(field, matrix, transpose):
    dims = (((2,), (0,)), ((), ())) if transpose else (((2,), (1,)), ((), ()))
    return lax.dot_general(field, matrix, dims, precision=HIGH)


def along_y(matrix, field, transpose):
    dims = (((0,), (0,)), ((), ())) if transpose else (((1,), (0,)), ((), ()))
    return lax.dot_general(matrix, field, dims, precision=HIGH)


def block_to_x(*fields):
    joined = jnp.concatenate(fields, axis=2)
    lines = lax.all_to_all(joined, "px", split_axis=1, concat_axis=0, tiled=True)
    depth = fields[0].shape[2]
    return [jnp.transpose(lines[:, :, k * depth:(k + 1) * depth], (2, 1, 0)) for k in range(len(fields))]


def x_to_block(*fields):
    joined = jnp.concatenate([jnp.transpose(f, (2, 1, 0)) for f in fields], axis=2)
    block = lax.all_to_all(joined, "px", split_axis=0, concat_axis=1, tiled=True)
    depth = fields[0].shape[0]
    return [block[:, :, k * depth:(k + 1) * depth] for k in range(len(fields))]


def x_to_y(*fields):
    joined = jnp.concatenate(fields, axis=2)
    lines = lax.all_to_all(joined, LINES, split_axis=0, concat_axis=0, tiled=True)
    lines = lines.reshape(-1, lines.shape[2])
    width = fields[0].shape[2]
    return [lines[:, k * width:(k + 1) * width] for k in range(len(fields))]


def y_to_x(*fields):
    joined = jnp.concatenate(fields, axis=1)
    count = lax.axis_size(LINES)
    joined = joined.reshape(count, -1, joined.shape[1])
    lines = lax.all_to_all(joined, LINES, split_axis=0, concat_axis=0, tiled=True)
    width = fields[0].shape[1]
    return [lines[:, :, k * width:(k + 1) * width] for k in range(len(fields))]


def local(initial, conduct, cotangent, inv_x, inv_y):
    first0 = initial + RATE * (halo_diff(initial, False) + zoperate_block(initial, conduct))
    f0x, cx, tx = block_to_x(first0, conduct, cotangent)
    half0 = along_x(f0x, inv_x, False)
    second0 = half0 + RATE * (xdiff(half0) + zoperate(half0, cx))
    s0y, ty = x_to_y(second0, tx)
    state1_y = along_y(inv_y, s0y, False)
    lam_second1_y = along_y(inv_y, ty, True)
    state1, ls1 = y_to_x(state1_y, lam_second1_y)
    first1 = state1 + RATE * (halo_diff(state1, True) + zoperate(state1, cx))
    half1 = along_x(first1, inv_x, False)
    grad = -RATE * zstep(ls1) * zstep(half1)
    lam_half1 = ls1 + RATE * (xdiff(ls1) + zoperate(ls1, cx))
    lam_first1 = along_x(lam_half1, inv_x, True)
    grad = grad - RATE * zstep(lam_first1) * zstep(state1)
    lam_state1 = lam_first1 + RATE * (halo_diff(lam_first1, True) + zoperate(lam_first1, cx))
    (lsy,) = x_to_y(lam_state1)
    lam_second0_y = along_y(inv_y, lsy, True)
    (ls0,) = y_to_x(lam_second0_y)
    grad = grad - RATE * zstep(ls0) * zstep(half0)
    lam_half0 = ls0 + RATE * (xdiff(ls0) + zoperate(ls0, cx))
    lam_first0 = along_x(lam_half0, inv_x, True)
    lf0, gb = x_to_block(lam_first0, grad)
    gradient = gb - RATE * zstep_block(lf0) * zstep_block(initial)
    adjoint = lf0 + RATE * (halo_diff(lf0, False) + zoperate_block(lf0, conduct))
    return (adjoint, gradient)


def solution(mesh):
    in_specs = (P("px", "py", None), P("px", "py", None), P("px", "py", None), P(), P())
    out_specs = (P("px", "py", None), P("px", "py", None))
    return jax.shard_map(local, mesh=mesh, in_specs=in_specs, out_specs=out_specs, check_vma=False)
```

```python
import jax
import jax.numpy as jnp
from jax import lax
from jax.sharding import PartitionSpec as P

RATE = 0.2
LINES = ("py", "px")
HIGH = lax.Precision.HIGHEST


def ydiff_block(field):
    count = lax.axis_size("py")
    below = lax.ppermute(field[:, -1:], "py", [(i, i + 1) for i in range(count - 1)])
    above = lax.ppermute(field[:, :1], "py", [(i + 1, i) for i in range(count - 1)])
    padded = jnp.concatenate([below, field, above], axis=1)
    return padded[:, 2:] + padded[:, :-2] - 2.0 * field


def zoperate_block(field, conduct):
    upper = jnp.concatenate([field[:, :, 1:], jnp.zeros_like(field[:, :, :1])], axis=2)
    flux = conduct * (upper - field)
    lower = jnp.concatenate([jnp.zeros_like(flux[:, :, :1]), flux[:, :, :-1]], axis=2)
    return flux - lower


def zstep_block(field):
    upper = jnp.concatenate([field[:, :, 1:], jnp.zeros_like(field[:, :, :1])], axis=2)
    return upper - field


def zstep(field):
    upper = jnp.concatenate([field[1:], jnp.zeros_like(field[:1])], axis=0)
    return upper - field


def zoperate(field, conduct):
    flux = conduct * zstep(field)
    lower = jnp.concatenate([jnp.zeros_like(flux[:1]), flux[:-1]], axis=0)
    return flux - lower


def xdiff(field):
    padded = jnp.pad(field, ((0, 0), (0, 0), (1, 1)))
    return padded[:, :, 2:] + padded[:, :, :-2] - 2.0 * field


def mesh_index(line):
    rows = lax.axis_size("px")
    cols = lax.axis_size("py")
    return (line % rows) * cols + line // rows


def ydiff(field):
    count = lax.axis_size(LINES)
    up = [(mesh_index(i), mesh_index(i + 1)) for i in range(count - 1)]
    down = [(b, a) for a, b in up]
    below = lax.ppermute(field[:, -1:], ("px", "py"), up)
    above = lax.ppermute(field[:, :1], ("px", "py"), down)
    padded = jnp.concatenate([below, field, above], axis=1)
    return padded[:, 2:] + padded[:, :-2] - 2.0 * field


def along_x(field, matrix, transpose):
    dims = (((2,), (0,)), ((), ())) if transpose else (((2,), (1,)), ((), ()))
    return lax.dot_general(field, matrix, dims, precision=HIGH)


def along_y(matrix, field, transpose):
    dims = (((0,), (0,)), ((), ())) if transpose else (((1,), (0,)), ((), ()))
    return lax.dot_general(matrix, field, dims, precision=HIGH)


def block_to_x(*fields):
    joined = jnp.concatenate(fields, axis=2)
    lines = lax.all_to_all(joined, "px", split_axis=1, concat_axis=0, tiled=True)
    depth = fields[0].shape[2]
    return [jnp.transpose(lines[:, :, k * depth:(k + 1) * depth], (2, 1, 0)) for k in range(len(fields))]


def x_to_block(*fields):
    joined = jnp.concatenate([jnp.transpose(f, (2, 1, 0)) for f in fields], axis=2)
    block = lax.all_to_all(joined, "px", split_axis=0, concat_axis=1, tiled=True)
    depth = fields[0].shape[0]
    return [block[:, :, k * depth:(k + 1) * depth] for k in range(len(fields))]


def x_to_y(*fields):
    joined = jnp.concatenate(fields, axis=2)
    lines = lax.all_to_all(joined, LINES, split_axis=0, concat_axis=0, tiled=True)
    lines = lines.reshape(-1, lines.shape[2])
    width = fields[0].shape[2]
    return [lines[:, k * width:(k + 1) * width] for k in range(len(fields))]


def y_to_x(*fields):
    joined = jnp.concatenate(fields, axis=1)
    count = lax.axis_size(LINES)
    joined = joined.reshape(count, -1, joined.shape[1])
    lines = lax.all_to_all(joined, LINES, split_axis=0, concat_axis=0, tiled=True)
    width = fields[0].shape[1]
    return [lines[:, :, k * width:(k + 1) * width] for k in range(len(fields))]


def block_planes(field):
    count = lax.axis_size(LINES)
    planes = jnp.transpose(field, (2, 1, 0))
    return planes.reshape(count, -1, field.shape[0] * field.shape[1] * field.shape[2] // count // 8)


def planes_to_y(pieces, block):
    rows = lax.axis_size("px")
    cols = lax.axis_size("py")
    depth, width = block[0], block[1]
    tiles = pieces.reshape(cols, rows, width, depth)
    return jnp.transpose(tiles, (0, 2, 1, 3)).reshape(cols * width, rows * depth)


def local(initial, conduct, cotangent, inv_x, inv_y):
    first0 = initial + RATE * (ydiff_block(initial) + zoperate_block(initial, conduct))
    f0x, cx = block_to_x(first0, conduct)
    half0 = along_x(f0x, inv_x, False)
    second0 = half0 + RATE * (xdiff(half0) + zoperate(half0, cx))
    s0y, tp = x_to_y(second0, block_planes(cotangent))
    ty = planes_to_y(tp, (initial.shape[0], initial.shape[1]))
    state1_y = along_y(inv_y, s0y, False)
    lam_second1_y = along_y(inv_y, ty, True)
    state1, ls1 = y_to_x(state1_y, lam_second1_y)
    first1 = state1 + RATE * (ydiff(state1) + zoperate(state1, cx))
    half1 = along_x(first1, inv_x, False)
    grad = -RATE * zstep(ls1) * zstep(half1)
    lam_half1 = ls1 + RATE * (xdiff(ls1) + zoperate(ls1, cx))
    lam_first1 = along_x(lam_half1, inv_x, True)
    grad = grad - RATE * zstep(lam_first1) * zstep(state1)
    lam_state1 = lam_first1 + RATE * (ydiff(lam_first1) + zoperate(lam_first1, cx))
    (lsy,) = x_to_y(lam_state1)
    lam_second0_y = along_y(inv_y, lsy, True)
    (ls0,) = y_to_x(lam_second0_y)
    grad = grad - RATE * zstep(ls0) * zstep(half0)
    lam_half0 = ls0 + RATE * (xdiff(ls0) + zoperate(ls0, cx))
    lam_first0 = along_x(lam_half0, inv_x, True)
    lf0, gb = x_to_block(lam_first0, grad)
    gradient = gb - RATE * zstep_block(lf0) * zstep_block(initial)
    adjoint = lf0 + RATE * (ydiff_block(lf0) + zoperate_block(lf0, conduct))
    return (adjoint, gradient)


def solution(mesh):
    in_specs = (P("px", "py", None), P("px", "py", None), P("px", "py", None), P(), P())
    out_specs = (P("px", "py", None), P("px", "py", None))
    return jax.shard_map(local, mesh=mesh, in_specs=in_specs, out_specs=out_specs, check_vma=False)
```

```python
import jax
import jax.numpy as jnp
from jax import lax
from jax.sharding import PartitionSpec as P

RATE = 0.2
LINES = ("py", "px")
HIGH = lax.Precision.HIGH


def ydiff_block(field):
    count = lax.axis_size("py")
    below = lax.ppermute(field[:, -1:], "py", [(i, i + 1) for i in range(count - 1)])
    above = lax.ppermute(field[:, :1], "py", [(i + 1, i) for i in range(count - 1)])
    padded = jnp.concatenate([below, field, above], axis=1)
    return padded[:, 2:] + padded[:, :-2] - 2.0 * field


def zoperate_block(field, conduct):
    upper = jnp.concatenate([field[:, :, 1:], jnp.zeros_like(field[:, :, :1])], axis=2)
    flux = conduct * (upper - field)
    lower = jnp.concatenate([jnp.zeros_like(flux[:, :, :1]), flux[:, :, :-1]], axis=2)
    return flux - lower


def zstep_block(field):
    upper = jnp.concatenate([field[:, :, 1:], jnp.zeros_like(field[:, :, :1])], axis=2)
    return upper - field


def zstep(field):
    upper = jnp.concatenate([field[1:], jnp.zeros_like(field[:1])], axis=0)
    return upper - field


def zoperate(field, conduct):
    flux = conduct * zstep(field)
    lower = jnp.concatenate([jnp.zeros_like(flux[:1]), flux[:-1]], axis=0)
    return flux - lower


def xdiff(field):
    padded = jnp.pad(field, ((0, 0), (0, 0), (1, 1)))
    return padded[:, :, 2:] + padded[:, :, :-2] - 2.0 * field


def mesh_index(line):
    rows = lax.axis_size("px")
    cols = lax.axis_size("py")
    return (line % rows) * cols + line // rows


def ydiff(field):
    count = lax.axis_size(LINES)
    up = [(mesh_index(i), mesh_index(i + 1)) for i in range(count - 1)]
    down = [(b, a) for a, b in up]
    below = lax.ppermute(field[:, -1:], ("px", "py"), up)
    above = lax.ppermute(field[:, :1], ("px", "py"), down)
    padded = jnp.concatenate([below, field, above], axis=1)
    return padded[:, 2:] + padded[:, :-2] - 2.0 * field


def along_x(field, matrix, transpose):
    dims = (((2,), (0,)), ((), ())) if transpose else (((2,), (1,)), ((), ()))
    return lax.dot_general(field, matrix, dims, precision=HIGH)


def along_y(matrix, field, transpose):
    dims = (((0,), (0,)), ((), ())) if transpose else (((1,), (0,)), ((), ()))
    return lax.dot_general(matrix, field, dims, precision=HIGH)


def block_to_x(*fields):
    joined = jnp.concatenate(fields, axis=2)
    lines = lax.all_to_all(joined, "px", split_axis=1, concat_axis=0, tiled=True)
    depth = fields[0].shape[2]
    return [jnp.transpose(lines[:, :, k * depth:(k + 1) * depth], (2, 1, 0)) for k in range(len(fields))]


def x_to_block(*fields):
    joined = jnp.concatenate([jnp.transpose(f, (2, 1, 0)) for f in fields], axis=2)
    block = lax.all_to_all(joined, "px", split_axis=0, concat_axis=1, tiled=True)
    depth = fields[0].shape[0]
    return [block[:, :, k * depth:(k + 1) * depth] for k in range(len(fields))]


def x_to_y(*fields):
    joined = jnp.concatenate(fields, axis=2)
    lines = lax.all_to_all(joined, LINES, split_axis=0, concat_axis=0, tiled=True)
    lines = lines.reshape(-1, lines.shape[2])
    width = fields[0].shape[2]
    return [lines[:, k * width:(k + 1) * width] for k in range(len(fields))]


def y_to_x(*fields):
    joined = jnp.concatenate(fields, axis=1)
    count = lax.axis_size(LINES)
    joined = joined.reshape(count, -1, joined.shape[1])
    lines = lax.all_to_all(joined, LINES, split_axis=0, concat_axis=0, tiled=True)
    width = fields[0].shape[1]
    return [lines[:, :, k * width:(k + 1) * width] for k in range(len(fields))]


def block_planes(field):
    count = lax.axis_size(LINES)
    planes = jnp.transpose(field, (2, 1, 0))
    return planes.reshape(count, -1, field.shape[0] * field.shape[1] * field.shape[2] // count // 8)


def planes_to_y(pieces, block):
    rows = lax.axis_size("px")
    cols = lax.axis_size("py")
    depth, width = block[0], block[1]
    tiles = pieces.reshape(cols, rows, width, depth)
    return jnp.transpose(tiles, (0, 2, 1, 3)).reshape(cols * width, rows * depth)


def local(initial, conduct, cotangent, inv_x, inv_y):
    first0 = initial + RATE * (ydiff_block(initial) + zoperate_block(initial, conduct))
    f0x, cx = block_to_x(first0, conduct)
    half0 = along_x(f0x, inv_x, False)
    second0 = half0 + RATE * (xdiff(half0) + zoperate(half0, cx))
    s0y, tp = x_to_y(second0, block_planes(cotangent))
    ty = planes_to_y(tp, (initial.shape[0], initial.shape[1]))
    state1_y = along_y(inv_y, s0y, False)
    lam_second1_y = along_y(inv_y, ty, True)
    state1, ls1 = y_to_x(state1_y, lam_second1_y)
    first1 = state1 + RATE * (ydiff(state1) + zoperate(state1, cx))
    half1 = along_x(first1, inv_x, False)
    grad = -RATE * zstep(ls1) * zstep(half1)
    lam_half1 = ls1 + RATE * (xdiff(ls1) + zoperate(ls1, cx))
    lam_first1 = along_x(lam_half1, inv_x, True)
    grad = grad - RATE * zstep(lam_first1) * zstep(state1)
    lam_state1 = lam_first1 + RATE * (ydiff(lam_first1) + zoperate(lam_first1, cx))
    (lsy,) = x_to_y(lam_state1)
    lam_second0_y = along_y(inv_y, lsy, True)
    (ls0,) = y_to_x(lam_second0_y)
    grad = grad - RATE * zstep(ls0) * zstep(half0)
    lam_half0 = ls0 + RATE * (xdiff(ls0) + zoperate(ls0, cx))
    lam_first0 = along_x(lam_half0, inv_x, True)
    lf0, gb = x_to_block(lam_first0, grad)
    gradient = gb - RATE * zstep_block(lf0) * zstep_block(initial)
    adjoint = lf0 + RATE * (ydiff_block(lf0) + zoperate_block(lf0, conduct))
    return (adjoint, gradient)


def solution(mesh):
    in_specs = (P("px", "py", None), P("px", "py", None), P("px", "py", None), P(), P())
    out_specs = (P("px", "py", None), P("px", "py", None))
    return jax.shard_map(local, mesh=mesh, in_specs=in_specs, out_specs=out_specs, check_vma=False)
```

```python
import functools

import jax
import jax.numpy as jnp
from jax import lax
from jax.experimental import pallas as pl
from jax.sharding import PartitionSpec as P

RATE = 0.2
LINES = ("py", "px")
HIGH = lax.Precision.HIGH


def ydiff_block(field):
    count = lax.axis_size("py")
    below = lax.ppermute(field[:, -1:], "py", [(i, i + 1) for i in range(count - 1)])
    above = lax.ppermute(field[:, :1], "py", [(i + 1, i) for i in range(count - 1)])
    padded = jnp.concatenate([below, field, above], axis=1)
    return padded[:, 2:] + padded[:, :-2] - 2.0 * field


def zoperate_block(field, conduct):
    upper = jnp.concatenate([field[:, :, 1:], jnp.zeros_like(field[:, :, :1])], axis=2)
    flux = conduct * (upper - field)
    lower = jnp.concatenate([jnp.zeros_like(flux[:, :, :1]), flux[:, :, :-1]], axis=2)
    return flux - lower


def zstep_block(field):
    upper = jnp.concatenate([field[:, :, 1:], jnp.zeros_like(field[:, :, :1])], axis=2)
    return upper - field


def zstep(field):
    upper = jnp.concatenate([field[1:], jnp.zeros_like(field[:1])], axis=0)
    return upper - field


def zoperate(field, conduct):
    flux = conduct * zstep(field)
    lower = jnp.concatenate([jnp.zeros_like(flux[:1]), flux[:-1]], axis=0)
    return flux - lower


def xdiff(field):
    padded = jnp.pad(field, ((0, 0), (0, 0), (1, 1)))
    return padded[:, :, 2:] + padded[:, :, :-2] - 2.0 * field


def mesh_index(line):
    rows = lax.axis_size("px")
    cols = lax.axis_size("py")
    return (line % rows) * cols + line // rows


def ydiff(field):
    count = lax.axis_size(LINES)
    up = [(mesh_index(i), mesh_index(i + 1)) for i in range(count - 1)]
    down = [(b, a) for a, b in up]
    below = lax.ppermute(field[:, -1:], ("px", "py"), up)
    above = lax.ppermute(field[:, :1], ("px", "py"), down)
    padded = jnp.concatenate([below, field, above], axis=1)
    return padded[:, 2:] + padded[:, :-2] - 2.0 * field


def along_x(field, matrix, transpose):
    dims = (((2,), (0,)), ((), ())) if transpose else (((2,), (1,)), ((), ()))
    return lax.dot_general(field, matrix, dims, precision=HIGH)


def block_to_x(*fields):
    joined = jnp.concatenate(fields, axis=2)
    lines = lax.all_to_all(joined, "px", split_axis=1, concat_axis=0, tiled=True)
    depth = fields[0].shape[2]
    return [jnp.transpose(lines[:, :, k * depth:(k + 1) * depth], (2, 1, 0)) for k in range(len(fields))]


def x_to_block(*fields):
    joined = jnp.concatenate([jnp.transpose(f, (2, 1, 0)) for f in fields], axis=2)
    block = lax.all_to_all(joined, "px", split_axis=0, concat_axis=1, tiled=True)
    depth = fields[0].shape[0]
    return [block[:, :, k * depth:(k + 1) * depth] for k in range(len(fields))]


def x_to_y(*fields):
    joined = jnp.concatenate(fields, axis=2)
    lines = lax.all_to_all(joined, LINES, split_axis=0, concat_axis=0, tiled=True)
    lines = lines.reshape(-1, lines.shape[2])
    width = fields[0].shape[2]
    return [lines[:, k * width:(k + 1) * width] for k in range(len(fields))]


def y_to_x(joined, parts):
    count = lax.axis_size(LINES)
    joined = joined.reshape(count, -1, joined.shape[1])
    lines = lax.all_to_all(joined, LINES, split_axis=0, concat_axis=0, tiled=True)
    width = joined.shape[2] // parts
    return [lines[:, :, k * width:(k + 1) * width] for k in range(parts)]


def block_planes(field):
    count = lax.axis_size(LINES)
    planes = jnp.transpose(field, (2, 1, 0))
    return planes.reshape(count, -1, field.shape[0] * field.shape[1] * field.shape[2] // count // 8)


def planes_to_y(pieces, block):
    rows = lax.axis_size("px")
    cols = lax.axis_size("py")
    depth, width = block[0], block[1]
    tiles = pieces.reshape(cols, rows, width, depth)
    return jnp.transpose(tiles, (0, 2, 1, 3)).reshape(cols * width, rows * depth)


def split(value):
    high = lax.reduce_precision(value, exponent_bits=8, mantissa_bits=7)
    return high.astype(jnp.bfloat16), (value - high).astype(jnp.bfloat16)


def _ymm_kernel(count, *refs):
    out = refs[-1]
    for k in range(count):
        high, low, f_high, f_low = refs[4 * k:4 * k + 4]
        a_high = high[...]
        top = f_high[...]
        acc = jnp.dot(a_high, top, preferred_element_type=jnp.float32)
        acc = acc + jnp.dot(a_high, f_low[...], preferred_element_type=jnp.float32)
        acc = acc + jnp.dot(low[...], top, preferred_element_type=jnp.float32)
        width = top.shape[1]
        out[:, k * width:(k + 1) * width] = acc


def y_products(*pairs):
    count = len(pairs)
    size, width = pairs[0][1].shape
    step = 256
    operands, specs = [], []
    for (high, low), field in pairs:
        operands += [high, low, *split(field)]
        specs += [
            pl.BlockSpec((step, size), lambda i: (i, 0)),
            pl.BlockSpec((step, size), lambda i: (i, 0)),
            pl.BlockSpec((size, width), lambda i: (0, 0)),
            pl.BlockSpec((size, width), lambda i: (0, 0)),
        ]
    flops = 6 * size * size * width * count
    return pl.pallas_call(
        functools.partial(_ymm_kernel, count),
        grid=(size // step,),
        out_shape=jax.ShapeDtypeStruct((size, width * count), jnp.float32),
        in_specs=specs,
        out_specs=pl.BlockSpec((step, width * count), lambda i: (i, 0)),
        cost_estimate=pl.CostEstimate(flops=flops, transcendentals=0, bytes_accessed=count * (4 * size * size + 8 * size * width)),
    )(*operands)


def local(initial, conduct, cotangent, inv_x, inv_y):
    forward_y = split(inv_y)
    backward_y = split(jnp.transpose(inv_y))
    first0 = initial + RATE * (ydiff_block(initial) + zoperate_block(initial, conduct))
    f0x, cx = block_to_x(first0, conduct)
    half0 = along_x(f0x, inv_x, False)
    second0 = half0 + RATE * (xdiff(half0) + zoperate(half0, cx))
    s0y, tp = x_to_y(second0, block_planes(cotangent))
    ty = planes_to_y(tp, (initial.shape[0], initial.shape[1]))
    joined = y_products((forward_y, s0y), (backward_y, ty))
    state1, ls1 = y_to_x(joined, 2)
    first1 = state1 + RATE * (ydiff(state1) + zoperate(state1, cx))
    half1 = along_x(first1, inv_x, False)
    grad = -RATE * zstep(ls1) * zstep(half1)
    lam_half1 = ls1 + RATE * (xdiff(ls1) + zoperate(ls1, cx))
    lam_first1 = along_x(lam_half1, inv_x, True)
    grad = grad - RATE * zstep(lam_first1) * zstep(state1)
    lam_state1 = lam_first1 + RATE * (ydiff(lam_first1) + zoperate(lam_first1, cx))
    (lsy,) = x_to_y(lam_state1)
    lam_second0_y = y_products((backward_y, lsy))
    (ls0,) = y_to_x(lam_second0_y, 1)
    grad = grad - RATE * zstep(ls0) * zstep(half0)
    lam_half0 = ls0 + RATE * (xdiff(ls0) + zoperate(ls0, cx))
    lam_first0 = along_x(lam_half0, inv_x, True)
    lf0, gb = x_to_block(lam_first0, grad)
    gradient = gb - RATE * zstep_block(lf0) * zstep_block(initial)
    adjoint = lf0 + RATE * (ydiff_block(lf0) + zoperate_block(lf0, conduct))
    return (adjoint, gradient)


def solution(mesh):
    in_specs = (P("px", "py", None), P("px", "py", None), P("px", "py", None), P(), P())
    out_specs = (P("px", "py", None), P("px", "py", None))
    return jax.shard_map(local, mesh=mesh, in_specs=in_specs, out_specs=out_specs, check_vma=False)
```

```python
import jax
import jax.numpy as jnp
from jax import lax
from jax.sharding import PartitionSpec as P

RATE = 0.2
LINES = ("py", "px")
HIGH = lax.Precision.HIGH


def ydiff_block(field):
    count = lax.axis_size("py")
    below = lax.ppermute(field[:, -1:], "py", [(i, i + 1) for i in range(count - 1)])
    above = lax.ppermute(field[:, :1], "py", [(i + 1, i) for i in range(count - 1)])
    padded = jnp.concatenate([below, field, above], axis=1)
    return padded[:, 2:] + padded[:, :-2] - 2.0 * field


def zoperate_block(field, conduct):
    upper = jnp.concatenate([field[:, :, 1:], jnp.zeros_like(field[:, :, :1])], axis=2)
    flux = conduct * (upper - field)
    lower = jnp.concatenate([jnp.zeros_like(flux[:, :, :1]), flux[:, :, :-1]], axis=2)
    return flux - lower


def zstep_block(field):
    upper = jnp.concatenate([field[:, :, 1:], jnp.zeros_like(field[:, :, :1])], axis=2)
    return upper - field


def zstep(field):
    upper = jnp.concatenate([field[1:], jnp.zeros_like(field[:1])], axis=0)
    return upper - field


def zoperate(field, conduct):
    flux = conduct * zstep(field)
    lower = jnp.concatenate([jnp.zeros_like(flux[:1]), flux[:-1]], axis=0)
    return flux - lower


def xdiff(field):
    padded = jnp.pad(field, ((0, 0), (0, 0), (1, 1)))
    return padded[:, :, 2:] + padded[:, :, :-2] - 2.0 * field


def mesh_index(line):
    rows = lax.axis_size("px")
    cols = lax.axis_size("py")
    return (line % rows) * cols + line // rows


def ydiff(*fields):
    count = lax.axis_size(LINES)
    up = [(mesh_index(i), mesh_index(i + 1)) for i in range(count - 1)]
    down = [(b, a) for a, b in up]
    depth = fields[0].shape[0]
    below = lax.ppermute(jnp.concatenate([f[:, -1:] for f in fields]), ("px", "py"), up)
    above = lax.ppermute(jnp.concatenate([f[:, :1] for f in fields]), ("px", "py"), down)
    diffs = []
    for k, field in enumerate(fields):
        edge = slice(k * depth, (k + 1) * depth)
        padded = jnp.concatenate([below[edge], field, above[edge]], axis=1)
        diffs.append(padded[:, 2:] + padded[:, :-2] - 2.0 * field)
    return diffs


def along_x(field, matrix, transpose):
    dims = (((2,), (0,)), ((), ())) if transpose else (((2,), (1,)), ((), ()))
    return lax.dot_general(field, matrix, dims, precision=HIGH)


def along_y(matrix, field, transpose):
    dims = (((0,), (0,)), ((), ())) if transpose else (((1,), (0,)), ((), ()))
    return lax.dot_general(matrix, field, dims, precision=HIGH)


def block_to_x(*fields):
    joined = jnp.concatenate(fields, axis=2)
    lines = lax.all_to_all(joined, "px", split_axis=1, concat_axis=0, tiled=True)
    depth = fields[0].shape[2]
    return [jnp.transpose(lines[:, :, k * depth:(k + 1) * depth], (2, 1, 0)) for k in range(len(fields))]


def x_to_block(*fields):
    joined = jnp.concatenate([jnp.transpose(f, (2, 1, 0)) for f in fields], axis=2)
    block = lax.all_to_all(joined, "px", split_axis=0, concat_axis=1, tiled=True)
    depth = fields[0].shape[0]
    return [block[:, :, k * depth:(k + 1) * depth] for k in range(len(fields))]


def x_to_y(*fields):
    joined = jnp.concatenate(fields, axis=2)
    lines = lax.all_to_all(joined, LINES, split_axis=0, concat_axis=0, tiled=True)
    lines = lines.reshape(-1, lines.shape[2])
    width = fields[0].shape[2]
    return [lines[:, k * width:(k + 1) * width] for k in range(len(fields))]


def y_to_x(*fields):
    joined = jnp.concatenate(fields, axis=1)
    count = lax.axis_size(LINES)
    joined = joined.reshape(count, -1, joined.shape[1])
    lines = lax.all_to_all(joined, LINES, split_axis=0, concat_axis=0, tiled=True)
    width = fields[0].shape[1]
    return [lines[:, :, k * width:(k + 1) * width] for k in range(len(fields))]


def block_planes(field):
    count = lax.axis_size(LINES)
    planes = jnp.transpose(field, (2, 1, 0))
    return planes.reshape(count, -1, field.shape[0] * field.shape[1] * field.shape[2] // count // 8)


def planes_to_y(pieces, block):
    rows = lax.axis_size("px")
    cols = lax.axis_size("py")
    depth, width = block[0], block[1]
    tiles = pieces.reshape(cols, rows, width, depth)
    return jnp.transpose(tiles, (0, 2, 1, 3)).reshape(cols * width, rows * depth)


def local(initial, conduct, cotangent, inv_x, inv_y):
    first0 = initial + RATE * (ydiff_block(initial) + zoperate_block(initial, conduct))
    f0x, cx = block_to_x(first0, conduct)
    half0 = along_x(f0x, inv_x, False)
    second0 = half0 + RATE * (xdiff(half0) + zoperate(half0, cx))
    s0y, tp = x_to_y(second0, block_planes(cotangent))
    ty = planes_to_y(tp, (initial.shape[0], initial.shape[1]))
    state1_y = along_y(inv_y, s0y, False)
    lam_second1_y = along_y(inv_y, ty, True)
    state1, ls1 = y_to_x(state1_y, lam_second1_y)
    lam_half1 = ls1 + RATE * (xdiff(ls1) + zoperate(ls1, cx))
    lam_first1 = along_x(lam_half1, inv_x, True)
    dy_state1, dy_lam_first1 = ydiff(state1, lam_first1)
    lam_state1 = lam_first1 + RATE * (dy_lam_first1 + zoperate(lam_first1, cx))
    first1 = state1 + RATE * (dy_state1 + zoperate(state1, cx))
    half1 = along_x(first1, inv_x, False)
    grad = -RATE * zstep(ls1) * zstep(half1)
    grad = grad - RATE * zstep(lam_first1) * zstep(state1)
    (lsy,) = x_to_y(lam_state1)
    lam_second0_y = along_y(inv_y, lsy, True)
    (ls0,) = y_to_x(lam_second0_y)
    grad = grad - RATE * zstep(ls0) * zstep(half0)
    lam_half0 = ls0 + RATE * (xdiff(ls0) + zoperate(ls0, cx))
    lam_first0 = along_x(lam_half0, inv_x, True)
    lf0, gb = x_to_block(lam_first0, grad)
    gradient = gb - RATE * zstep_block(lf0) * zstep_block(initial)
    adjoint = lf0 + RATE * (ydiff_block(lf0) + zoperate_block(lf0, conduct))
    return (adjoint, gradient)


def solution(mesh):
    in_specs = (P("px", "py", None), P("px", "py", None), P("px", "py", None), P(), P())
    out_specs = (P("px", "py", None), P("px", "py", None))
    return jax.shard_map(local, mesh=mesh, in_specs=in_specs, out_specs=out_specs, check_vma=False)
```

```python
import jax
import jax.numpy as jnp
from jax import lax
from jax.sharding import PartitionSpec as P

RATE = 0.2
LINES = ("py", "px")
HIGH = lax.Precision.HIGH


def ydiff_block(field):
    count = lax.axis_size("py")
    below = lax.ppermute(field[:, -1:], "py", [(i, i + 1) for i in range(count - 1)])
    above = lax.ppermute(field[:, :1], "py", [(i + 1, i) for i in range(count - 1)])
    padded = jnp.concatenate([below, field, above], axis=1)
    return padded[:, 2:] + padded[:, :-2] - 2.0 * field


def zoperate_block(field, conduct):
    upper = jnp.concatenate([field[:, :, 1:], jnp.zeros_like(field[:, :, :1])], axis=2)
    flux = conduct * (upper - field)
    lower = jnp.concatenate([jnp.zeros_like(flux[:, :, :1]), flux[:, :, :-1]], axis=2)
    return flux - lower


def zstep_block(field):
    upper = jnp.concatenate([field[:, :, 1:], jnp.zeros_like(field[:, :, :1])], axis=2)
    return upper - field


def zstep(field):
    upper = jnp.concatenate([field[1:], jnp.zeros_like(field[:1])], axis=0)
    return upper - field


def zoperate(field, conduct):
    flux = conduct * zstep(field)
    lower = jnp.concatenate([jnp.zeros_like(flux[:1]), flux[:-1]], axis=0)
    return flux - lower


def xdiff(field):
    padded = jnp.pad(field, ((0, 0), (0, 0), (1, 1)))
    return padded[:, :, 2:] + padded[:, :, :-2] - 2.0 * field


def mesh_index(line):
    rows = lax.axis_size("px")
    cols = lax.axis_size("py")
    return (line % rows) * cols + line // rows


def ydiff(*fields):
    count = lax.axis_size(LINES)
    up = [(mesh_index(i), mesh_index(i + 1)) for i in range(count - 1)]
    down = [(b, a) for a, b in up]
    depth = fields[0].shape[0]
    below = lax.ppermute(jnp.concatenate([f[:, -1:] for f in fields]), ("px", "py"), up)
    above = lax.ppermute(jnp.concatenate([f[:, :1] for f in fields]), ("px", "py"), down)
    diffs = []
    for k, field in enumerate(fields):
        edge = slice(k * depth, (k + 1) * depth)
        padded = jnp.concatenate([below[edge], field, above[edge]], axis=1)
        diffs.append(padded[:, 2:] + padded[:, :-2] - 2.0 * field)
    return diffs


def along_x(field, matrix, transpose):
    dims = (((2,), (0,)), ((), ())) if transpose else (((2,), (1,)), ((), ()))
    return lax.dot_general(field, matrix, dims, precision=HIGH)


def along_y(matrix, field, transpose):
    dims = (((0,), (0,)), ((), ())) if transpose else (((1,), (0,)), ((), ()))
    return lax.dot_general(matrix, field, dims, precision=HIGH)


def block_to_x(*fields):
    joined = jnp.concatenate(fields, axis=2)
    lines = lax.all_to_all(joined, "px", split_axis=1, concat_axis=0, tiled=True)
    depth = fields[0].shape[2]
    return [jnp.transpose(lines[:, :, k * depth:(k + 1) * depth], (2, 1, 0)) for k in range(len(fields))]


def x_to_block(*fields):
    joined = jnp.concatenate([jnp.transpose(f, (2, 1, 0)) for f in fields], axis=2)
    block = lax.all_to_all(joined, "px", split_axis=0, concat_axis=1, tiled=True)
    depth = fields[0].shape[0]
    return [block[:, :, k * depth:(k + 1) * depth] for k in range(len(fields))]


def x_to_y(*fields):
    joined = jnp.concatenate(fields, axis=2)
    lines = lax.all_to_all(joined, LINES, split_axis=0, concat_axis=0, tiled=True)
    lines = lines.reshape(-1, lines.shape[2])
    width = fields[0].shape[2]
    return [lines[:, k * width:(k + 1) * width] for k in range(len(fields))]


def y_to_x(*fields):
    joined = jnp.concatenate(fields, axis=1)
    count = lax.axis_size(LINES)
    joined = joined.reshape(count, -1, joined.shape[1])
    lines = lax.all_to_all(joined, LINES, split_axis=0, concat_axis=0, tiled=True)
    width = fields[0].shape[1]
    return [lines[:, :, k * width:(k + 1) * width] for k in range(len(fields))]


def block_planes(field):
    count = lax.axis_size(LINES)
    planes = jnp.transpose(field, (2, 1, 0))
    return planes.reshape(count, -1, field.shape[0] * field.shape[1] * field.shape[2] // count // 8)


def planes_to_y(pieces, block):
    rows = lax.axis_size("px")
    cols = lax.axis_size("py")
    depth, width = block[0], block[1]
    tiles = pieces.reshape(cols, rows, width, depth)
    return jnp.transpose(tiles, (0, 2, 1, 3)).reshape(cols * width, rows * depth)


def local(initial, conduct, cotangent, inv_x, inv_y):
    (tp,) = x_to_y(block_planes(cotangent))
    ty = planes_to_y(tp, (initial.shape[0], initial.shape[1]))
    lam_second1_y = along_y(inv_y, ty, True)
    first0 = initial + RATE * (ydiff_block(initial) + zoperate_block(initial, conduct))
    f0x, cx = block_to_x(first0, conduct)
    half0 = along_x(f0x, inv_x, False)
    second0 = half0 + RATE * (xdiff(half0) + zoperate(half0, cx))
    (s0y,) = x_to_y(second0)
    state1_y = along_y(inv_y, s0y, False)
    state1, ls1 = y_to_x(state1_y, lam_second1_y)
    lam_half1 = ls1 + RATE * (xdiff(ls1) + zoperate(ls1, cx))
    lam_first1 = along_x(lam_half1, inv_x, True)
    dy_state1, dy_lam_first1 = ydiff(state1, lam_first1)
    lam_state1 = lam_first1 + RATE * (dy_lam_first1 + zoperate(lam_first1, cx))
    first1 = state1 + RATE * (dy_state1 + zoperate(state1, cx))
    half1 = along_x(first1, inv_x, False)
    grad = -RATE * zstep(ls1) * zstep(half1)
    grad = grad - RATE * zstep(lam_first1) * zstep(state1)
    (lsy,) = x_to_y(lam_state1)
    lam_second0_y = along_y(inv_y, lsy, True)
    (ls0,) = y_to_x(lam_second0_y)
    grad = grad - RATE * zstep(ls0) * zstep(half0)
    lam_half0 = ls0 + RATE * (xdiff(ls0) + zoperate(ls0, cx))
    lam_first0 = along_x(lam_half0, inv_x, True)
    lf0, gb = x_to_block(lam_first0, grad)
    gradient = gb - RATE * zstep_block(lf0) * zstep_block(initial)
    adjoint = lf0 + RATE * (ydiff_block(lf0) + zoperate_block(lf0, conduct))
    return (adjoint, gradient)


def solution(mesh):
    in_specs = (P("px", "py", None), P("px", "py", None), P("px", "py", None), P(), P())
    out_specs = (P("px", "py", None), P("px", "py", None))
    return jax.shard_map(local, mesh=mesh, in_specs=in_specs, out_specs=out_specs, check_vma=False)
```

```python
import jax
import jax.numpy as jnp
from jax import lax
from jax.sharding import PartitionSpec as P

RATE = 0.2
LINES = ("py", "px")
HIGH = lax.Precision.HIGH


def ydiff_block(field):
    count = lax.axis_size("py")
    below = lax.ppermute(field[:, -1:], "py", [(i, i + 1) for i in range(count - 1)])
    above = lax.ppermute(field[:, :1], "py", [(i + 1, i) for i in range(count - 1)])
    padded = jnp.concatenate([below, field, above], axis=1)
    return padded[:, 2:] + padded[:, :-2] - 2.0 * field


def zoperate_block(field, conduct):
    upper = jnp.concatenate([field[:, :, 1:], jnp.zeros_like(field[:, :, :1])], axis=2)
    flux = conduct * (upper - field)
    lower = jnp.concatenate([jnp.zeros_like(flux[:, :, :1]), flux[:, :, :-1]], axis=2)
    return flux - lower


def zstep_block(field):
    upper = jnp.concatenate([field[:, :, 1:], jnp.zeros_like(field[:, :, :1])], axis=2)
    return upper - field


def zstep(field):
    upper = jnp.concatenate([field[1:], jnp.zeros_like(field[:1])], axis=0)
    return upper - field


def zoperate(field, conduct):
    flux = conduct * zstep(field)
    lower = jnp.concatenate([jnp.zeros_like(flux[:1]), flux[:-1]], axis=0)
    return flux - lower


def xdiff(field):
    padded = jnp.pad(field, ((0, 0), (0, 0), (1, 1)))
    return padded[:, :, 2:] + padded[:, :, :-2] - 2.0 * field


def mesh_index(line):
    rows = lax.axis_size("px")
    cols = lax.axis_size("py")
    return (line % rows) * cols + line // rows


def ydiff(*fields):
    count = lax.axis_size(LINES)
    up = [(mesh_index(i), mesh_index(i + 1)) for i in range(count - 1)]
    down = [(b, a) for a, b in up]
    depth = fields[0].shape[0]
    below = lax.ppermute(jnp.concatenate([f[:, -1:] for f in fields]), ("px", "py"), up)
    above = lax.ppermute(jnp.concatenate([f[:, :1] for f in fields]), ("px", "py"), down)
    diffs = []
    for k, field in enumerate(fields):
        edge = slice(k * depth, (k + 1) * depth)
        padded = jnp.concatenate([below[edge], field, above[edge]], axis=1)
        diffs.append(padded[:, 2:] + padded[:, :-2] - 2.0 * field)
    return diffs


def along_x(field, matrix, transpose):
    dims = (((2,), (0,)), ((), ())) if transpose else (((2,), (1,)), ((), ()))
    return lax.dot_general(field, matrix, dims, precision=HIGH)


def along_y(matrix, field, transpose):
    dims = (((0,), (0,)), ((), ())) if transpose else (((1,), (0,)), ((), ()))
    return lax.dot_general(matrix, field, dims, precision=HIGH)


def block_to_x(*fields):
    joined = jnp.concatenate(fields, axis=2)
    lines = lax.all_to_all(joined, "px", split_axis=1, concat_axis=0, tiled=True)
    depth = fields[0].shape[2]
    return [jnp.transpose(lines[:, :, k * depth:(k + 1) * depth], (2, 1, 0)) for k in range(len(fields))]


def x_to_block(*fields):
    joined = jnp.concatenate([jnp.transpose(f, (2, 1, 0)) for f in fields], axis=2)
    block = lax.all_to_all(joined, "px", split_axis=0, concat_axis=1, tiled=True)
    depth = fields[0].shape[0]
    return [block[:, :, k * depth:(k + 1) * depth] for k in range(len(fields))]


def x_to_y(*fields):
    joined = jnp.concatenate(fields, axis=2)
    lines = lax.all_to_all(joined, LINES, split_axis=0, concat_axis=0, tiled=True)
    lines = lines.reshape(-1, lines.shape[2])
    width = fields[0].shape[2]
    return [lines[:, k * width:(k + 1) * width] for k in range(len(fields))]


def y_to_x(*fields):
    joined = jnp.concatenate(fields, axis=1)
    count = lax.axis_size(LINES)
    joined = joined.reshape(count, -1, joined.shape[1])
    lines = lax.all_to_all(joined, LINES, split_axis=0, concat_axis=0, tiled=True)
    width = fields[0].shape[1]
    return [lines[:, :, k * width:(k + 1) * width] for k in range(len(fields))]


def block_planes(field):
    count = lax.axis_size(LINES)
    planes = jnp.transpose(field, (2, 1, 0))
    return planes.reshape(count, -1, field.shape[0] * field.shape[1] * field.shape[2] // count // 8)


def planes_to_y(pieces, block):
    rows = lax.axis_size("px")
    cols = lax.axis_size("py")
    depth, width = block[0], block[1]
    tiles = pieces.reshape(cols, rows, width, depth)
    return jnp.transpose(tiles, (0, 2, 1, 3)).reshape(cols * width, rows * depth)


def local(initial, conduct, cotangent, inv_x, inv_y):
    (tp,) = x_to_y(block_planes(cotangent))
    ty = planes_to_y(tp, (initial.shape[0], initial.shape[1]))
    lam_second1_y = along_y(inv_y, ty, True)
    first0 = initial + RATE * (ydiff_block(initial) + zoperate_block(initial, conduct))
    f0x, cx = block_to_x(first0, conduct)
    half0 = along_x(f0x, inv_x, False)
    second0 = half0 + RATE * (xdiff(half0) + zoperate(half0, cx))
    count = lax.axis_size(LINES)
    s0y, ls1 = x_to_y(second0, lam_second1_y.reshape(count, -1, lam_second1_y.shape[1]))
    ls1 = ls1.reshape(second0.shape)
    state1_y = along_y(inv_y, s0y, False)
    (state1,) = y_to_x(state1_y)
    lam_half1 = ls1 + RATE * (xdiff(ls1) + zoperate(ls1, cx))
    lam_first1 = along_x(lam_half1, inv_x, True)
    (dy_lam_first1,) = ydiff(lam_first1)
    (dy_state1,) = ydiff(state1)
    lam_state1 = lam_first1 + RATE * (dy_lam_first1 + zoperate(lam_first1, cx))
    first1 = state1 + RATE * (dy_state1 + zoperate(state1, cx))
    half1 = along_x(first1, inv_x, False)
    grad = -RATE * zstep(ls1) * zstep(half1)
    grad = grad - RATE * zstep(lam_first1) * zstep(state1)
    (lsy,) = x_to_y(lam_state1)
    lam_second0_y = along_y(inv_y, lsy, True)
    (ls0,) = y_to_x(lam_second0_y)
    grad = grad - RATE * zstep(ls0) * zstep(half0)
    lam_half0 = ls0 + RATE * (xdiff(ls0) + zoperate(ls0, cx))
    lam_first0 = along_x(lam_half0, inv_x, True)
    lf0, gb = x_to_block(lam_first0, grad)
    gradient = gb - RATE * zstep_block(lf0) * zstep_block(initial)
    adjoint = lf0 + RATE * (ydiff_block(lf0) + zoperate_block(lf0, conduct))
    return (adjoint, gradient)


def solution(mesh):
    in_specs = (P("px", "py", None), P("px", "py", None), P("px", "py", None), P(), P())
    out_specs = (P("px", "py", None), P("px", "py", None))
    return jax.shard_map(local, mesh=mesh, in_specs=in_specs, out_specs=out_specs, check_vma=False)
```

```python
import jax
import jax.numpy as jnp
from jax import lax
from jax.sharding import PartitionSpec as P

RATE = 0.2
LINES = ("py", "px")
HIGH = lax.Precision.HIGH


def ydiff_block(field):
    count = lax.axis_size("py")
    below = lax.ppermute(field[:, -1:], "py", [(i, i + 1) for i in range(count - 1)])
    above = lax.ppermute(field[:, :1], "py", [(i + 1, i) for i in range(count - 1)])
    padded = jnp.concatenate([below, field, above], axis=1)
    return padded[:, 2:] + padded[:, :-2] - 2.0 * field


def zoperate_block(field, conduct):
    upper = jnp.concatenate([field[:, :, 1:], jnp.zeros_like(field[:, :, :1])], axis=2)
    flux = conduct * (upper - field)
    lower = jnp.concatenate([jnp.zeros_like(flux[:, :, :1]), flux[:, :, :-1]], axis=2)
    return flux - lower


def zstep_block(field):
    upper = jnp.concatenate([field[:, :, 1:], jnp.zeros_like(field[:, :, :1])], axis=2)
    return upper - field


def zstep(field):
    upper = jnp.concatenate([field[1:], jnp.zeros_like(field[:1])], axis=0)
    return upper - field


def zoperate(field, conduct):
    flux = conduct * zstep(field)
    lower = jnp.concatenate([jnp.zeros_like(flux[:1]), flux[:-1]], axis=0)
    return flux - lower


def xdiff(field):
    padded = jnp.pad(field, ((0, 0), (0, 0), (1, 1)))
    return padded[:, :, 2:] + padded[:, :, :-2] - 2.0 * field


def mesh_index(line):
    rows = lax.axis_size("px")
    cols = lax.axis_size("py")
    return (line % rows) * cols + line // rows


def ydiff(*fields):
    count = lax.axis_size(LINES)
    up = [(mesh_index(i), mesh_index(i + 1)) for i in range(count - 1)]
    down = [(b, a) for a, b in up]
    depth = fields[0].shape[0]
    below = lax.ppermute(jnp.concatenate([f[:, -1:] for f in fields]), ("px", "py"), up)
    above = lax.ppermute(jnp.concatenate([f[:, :1] for f in fields]), ("px", "py"), down)
    diffs = []
    for k, field in enumerate(fields):
        edge = slice(k * depth, (k + 1) * depth)
        padded = jnp.concatenate([below[edge], field, above[edge]], axis=1)
        diffs.append(padded[:, 2:] + padded[:, :-2] - 2.0 * field)
    return diffs


def along_x(field, matrix, transpose):
    dims = (((2,), (0,)), ((), ())) if transpose else (((2,), (1,)), ((), ()))
    return lax.dot_general(field, matrix, dims, precision=HIGH)


def along_y(matrix, field, transpose):
    dims = (((0,), (0,)), ((), ())) if transpose else (((1,), (0,)), ((), ()))
    return lax.dot_general(matrix, field, dims, precision=HIGH)


def block_to_x(*fields):
    joined = jnp.concatenate(fields, axis=2)
    lines = lax.all_to_all(joined, "px", split_axis=1, concat_axis=0, tiled=True)
    depth = fields[0].shape[2]
    return [jnp.transpose(lines[:, :, k * depth:(k + 1) * depth], (2, 1, 0)) for k in range(len(fields))]


def x_to_block(*fields):
    joined = jnp.concatenate([jnp.transpose(f, (2, 1, 0)) for f in fields], axis=2)
    block = lax.all_to_all(joined, "px", split_axis=0, concat_axis=1, tiled=True)
    depth = fields[0].shape[0]
    return [block[:, :, k * depth:(k + 1) * depth] for k in range(len(fields))]


def x_to_y(*fields):
    joined = jnp.concatenate(fields, axis=2)
    lines = lax.all_to_all(joined, LINES, split_axis=0, concat_axis=0, tiled=True)
    lines = lines.reshape(-1, lines.shape[2])
    width = fields[0].shape[2]
    return [lines[:, k * width:(k + 1) * width] for k in range(len(fields))]


def y_to_x(*fields):
    joined = jnp.concatenate(fields, axis=1)
    count = lax.axis_size(LINES)
    joined = joined.reshape(count, -1, joined.shape[1])
    lines = lax.all_to_all(joined, LINES, split_axis=0, concat_axis=0, tiled=True)
    width = fields[0].shape[1]
    return [lines[:, :, k * width:(k + 1) * width] for k in range(len(fields))]


def block_planes(field):
    count = lax.axis_size(LINES)
    planes = jnp.transpose(field, (2, 1, 0))
    return planes.reshape(count, -1, field.shape[0] * field.shape[1] * field.shape[2] // count // 8)


def planes_to_y(pieces, block):
    rows = lax.axis_size("px")
    cols = lax.axis_size("py")
    depth, width = block[0], block[1]
    tiles = pieces.reshape(cols, rows, width, depth)
    return jnp.transpose(tiles, (0, 2, 1, 3)).reshape(cols * width, rows * depth)


def local(initial, conduct, cotangent, inv_x, inv_y):
    (tp,) = x_to_y(block_planes(cotangent))
    ty = planes_to_y(tp, (initial.shape[0], initial.shape[1]))
    lam_second1_y = along_y(inv_y, ty, True)
    first0 = initial + RATE * (ydiff_block(initial) + zoperate_block(initial, conduct))
    f0x, cx = block_to_x(first0, conduct)
    half0 = along_x(f0x, inv_x, False)
    second0 = half0 + RATE * (xdiff(half0) + zoperate(half0, cx))
    count = lax.axis_size(LINES)
    s0y, ls1 = x_to_y(second0, lam_second1_y.reshape(count, -1, lam_second1_y.shape[1]))
    ls1 = ls1.reshape(second0.shape)
    state1_y = along_y(inv_y, s0y, False)
    lam_half1 = ls1 + RATE * (xdiff(ls1) + zoperate(ls1, cx))
    lam_first1 = along_x(lam_half1, inv_x, True)
    (dy_lam_first1,) = ydiff(lam_first1)
    lam_state1 = lam_first1 + RATE * (dy_lam_first1 + zoperate(lam_first1, cx))
    lsy, state1 = x_to_y(lam_state1, state1_y.reshape(lam_state1.shape))
    state1 = state1.reshape(lam_state1.shape)
    (dy_state1,) = ydiff(state1)
    first1 = state1 + RATE * (dy_state1 + zoperate(state1, cx))
    half1 = along_x(first1, inv_x, False)
    grad = -RATE * zstep(ls1) * zstep(half1)
    grad = grad - RATE * zstep(lam_first1) * zstep(state1)
    lam_second0_y = along_y(inv_y, lsy, True)
    (ls0,) = y_to_x(lam_second0_y)
    grad = grad - RATE * zstep(ls0) * zstep(half0)
    lam_half0 = ls0 + RATE * (xdiff(ls0) + zoperate(ls0, cx))
    lam_first0 = along_x(lam_half0, inv_x, True)
    lf0, gb = x_to_block(lam_first0, grad)
    gradient = gb - RATE * zstep_block(lf0) * zstep_block(initial)
    adjoint = lf0 + RATE * (ydiff_block(lf0) + zoperate_block(lf0, conduct))
    return (adjoint, gradient)


def solution(mesh):
    in_specs = (P("px", "py", None), P("px", "py", None), P("px", "py", None), P(), P())
    out_specs = (P("px", "py", None), P("px", "py", None))
    return jax.shard_map(local, mesh=mesh, in_specs=in_specs, out_specs=out_specs, check_vma=False)
```

```python
import jax
import jax.numpy as jnp
from jax import lax
from jax.experimental.layout import Layout, with_layout_constraint
from jax.sharding import PartitionSpec as P

RATE = 0.2
LINES = ("py", "px")
HIGH = lax.Precision.HIGH


def ydiff_block(field):
    count = lax.axis_size("py")
    below = lax.ppermute(field[:, -1:], "py", [(i, i + 1) for i in range(count - 1)])
    above = lax.ppermute(field[:, :1], "py", [(i + 1, i) for i in range(count - 1)])
    padded = jnp.concatenate([below, field, above], axis=1)
    return padded[:, 2:] + padded[:, :-2] - 2.0 * field


def zoperate_block(field, conduct):
    upper = jnp.concatenate([field[:, :, 1:], jnp.zeros_like(field[:, :, :1])], axis=2)
    flux = conduct * (upper - field)
    lower = jnp.concatenate([jnp.zeros_like(flux[:, :, :1]), flux[:, :, :-1]], axis=2)
    return flux - lower


def zstep_block(field):
    upper = jnp.concatenate([field[:, :, 1:], jnp.zeros_like(field[:, :, :1])], axis=2)
    return upper - field


def zstep(field):
    upper = jnp.concatenate([field[1:], jnp.zeros_like(field[:1])], axis=0)
    return upper - field


def zoperate(field, conduct):
    flux = conduct * zstep(field)
    lower = jnp.concatenate([jnp.zeros_like(flux[:1]), flux[:-1]], axis=0)
    return flux - lower


def xdiff(field):
    padded = jnp.pad(field, ((0, 0), (0, 0), (1, 1)))
    return padded[:, :, 2:] + padded[:, :, :-2] - 2.0 * field


def mesh_index(line):
    rows = lax.axis_size("px")
    cols = lax.axis_size("py")
    return (line % rows) * cols + line // rows


def ydiff(*fields):
    count = lax.axis_size(LINES)
    up = [(mesh_index(i), mesh_index(i + 1)) for i in range(count - 1)]
    down = [(b, a) for a, b in up]
    depth = fields[0].shape[0]
    below = lax.ppermute(jnp.concatenate([f[:, -1:] for f in fields]), ("px", "py"), up)
    above = lax.ppermute(jnp.concatenate([f[:, :1] for f in fields]), ("px", "py"), down)
    diffs = []
    for k, field in enumerate(fields):
        edge = slice(k * depth, (k + 1) * depth)
        padded = jnp.concatenate([below[edge], field, above[edge]], axis=1)
        diffs.append(padded[:, 2:] + padded[:, :-2] - 2.0 * field)
    return diffs


def along_x(field, matrix, transpose):
    dims = (((2,), (0,)), ((), ())) if transpose else (((2,), (1,)), ((), ()))
    return lax.dot_general(field, matrix, dims, precision=HIGH)


def along_y(matrix, field, transpose):
    dims = (((0,), (0,)), ((), ())) if transpose else (((1,), (0,)), ((), ()))
    return lax.dot_general(matrix, field, dims, precision=HIGH)


def block_to_x(*fields):
    joined = jnp.concatenate(fields, axis=2)
    lines = lax.all_to_all(joined, "px", split_axis=1, concat_axis=0, tiled=True)
    depth = fields[0].shape[2]
    return [jnp.transpose(lines[:, :, k * depth:(k + 1) * depth], (2, 1, 0)) for k in range(len(fields))]


def x_to_block(*fields):
    joined = jnp.concatenate([jnp.transpose(f, (2, 1, 0)) for f in fields], axis=2)
    block = lax.all_to_all(joined, "px", split_axis=0, concat_axis=1, tiled=True)
    depth = fields[0].shape[0]
    return [block[:, :, k * depth:(k + 1) * depth] for k in range(len(fields))]


def x_to_y(*fields):
    joined = jnp.concatenate(fields, axis=2)
    lines = lax.all_to_all(joined, LINES, split_axis=0, concat_axis=0, tiled=True)
    lines = lines.reshape(-1, lines.shape[2])
    width = fields[0].shape[2]
    return [lines[:, k * width:(k + 1) * width] for k in range(len(fields))]


def y_to_x(*fields):
    joined = jnp.concatenate(fields, axis=1)
    count = lax.axis_size(LINES)
    joined = joined.reshape(count, -1, joined.shape[1])
    lines = lax.all_to_all(joined, LINES, split_axis=0, concat_axis=0, tiled=True)
    width = fields[0].shape[1]
    return [lines[:, :, k * width:(k + 1) * width] for k in range(len(fields))]


def block_planes(field):
    count = lax.axis_size(LINES)
    planes = jnp.transpose(field, (2, 1, 0))
    return planes.reshape(count, -1, field.shape[0] * field.shape[1] * field.shape[2] // count // 8)


def planes_to_y(pieces, block):
    rows = lax.axis_size("px")
    cols = lax.axis_size("py")
    depth, width = block[0], block[1]
    tiles = pieces.reshape(cols, rows, width, depth)
    return jnp.transpose(tiles, (0, 2, 1, 3)).reshape(cols * width, rows * depth)


def rows(field):
    return with_layout_constraint(field, Layout(tuple(range(field.ndim))))


def local(initial, conduct, cotangent, inv_x, inv_y):
    (tp,) = x_to_y(block_planes(cotangent))
    ty = planes_to_y(tp, (initial.shape[0], initial.shape[1]))
    lam_second1_y = along_y(inv_y, ty, True)
    first0 = initial + RATE * (ydiff_block(initial) + zoperate_block(initial, conduct))
    f0x, cx = block_to_x(first0, conduct)
    half0 = along_x(f0x, inv_x, False)
    second0 = half0 + RATE * (xdiff(half0) + zoperate(half0, cx))
    count = lax.axis_size(LINES)
    s0y, ls1 = x_to_y(second0, lam_second1_y.reshape(count, -1, lam_second1_y.shape[1]))
    ls1 = rows(ls1.reshape(second0.shape))
    state1_y = along_y(inv_y, s0y, False)
    lam_half1 = ls1 + RATE * (xdiff(ls1) + zoperate(ls1, cx))
    lam_first1 = along_x(lam_half1, inv_x, True)
    (dy_lam_first1,) = ydiff(lam_first1)
    lam_state1 = lam_first1 + RATE * (dy_lam_first1 + zoperate(lam_first1, cx))
    lsy, state1 = x_to_y(rows(lam_state1), state1_y.reshape(lam_state1.shape))
    state1 = rows(state1.reshape(lam_state1.shape))
    (dy_state1,) = ydiff(state1)
    first1 = state1 + RATE * (dy_state1 + zoperate(state1, cx))
    half1 = along_x(first1, inv_x, False)
    grad = -RATE * zstep(ls1) * zstep(half1)
    grad = grad - RATE * zstep(lam_first1) * zstep(state1)
    lam_second0_y = along_y(inv_y, lsy, True)
    (ls0,) = y_to_x(lam_second0_y)
    ls0 = rows(ls0)
    grad = grad - RATE * zstep(ls0) * zstep(half0)
    lam_half0 = ls0 + RATE * (xdiff(ls0) + zoperate(ls0, cx))
    lam_first0 = along_x(lam_half0, inv_x, True)
    lf0, gb = x_to_block(lam_first0, grad)
    gradient = gb - RATE * zstep_block(lf0) * zstep_block(initial)
    adjoint = lf0 + RATE * (ydiff_block(lf0) + zoperate_block(lf0, conduct))
    return (adjoint, gradient)


def solution(mesh):
    in_specs = (P("px", "py", None), P("px", "py", None), P("px", "py", None), P(), P())
    out_specs = (P("px", "py", None), P("px", "py", None))
    return jax.shard_map(local, mesh=mesh, in_specs=in_specs, out_specs=out_specs, check_vma=False)
```

```python
import jax
import jax.numpy as jnp
from jax import lax
from jax.experimental.layout import Layout, with_layout_constraint
from jax.sharding import PartitionSpec as P

RATE = 0.2
LINES = ("py", "px")
HIGH = lax.Precision.HIGH


def ydiff_block(field):
    count = lax.axis_size("py")
    below = lax.ppermute(field[:, -1:], "py", [(i, i + 1) for i in range(count - 1)])
    above = lax.ppermute(field[:, :1], "py", [(i + 1, i) for i in range(count - 1)])
    padded = jnp.concatenate([below, field, above], axis=1)
    return padded[:, 2:] + padded[:, :-2] - 2.0 * field


def zoperate_block(field, conduct):
    upper = jnp.concatenate([field[:, :, 1:], jnp.zeros_like(field[:, :, :1])], axis=2)
    flux = conduct * (upper - field)
    lower = jnp.concatenate([jnp.zeros_like(flux[:, :, :1]), flux[:, :, :-1]], axis=2)
    return flux - lower


def zstep_block(field):
    upper = jnp.concatenate([field[:, :, 1:], jnp.zeros_like(field[:, :, :1])], axis=2)
    return upper - field


def zstep(field):
    upper = jnp.concatenate([field[1:], jnp.zeros_like(field[:1])], axis=0)
    return upper - field


def zoperate(field, conduct):
    flux = conduct * zstep(field)
    lower = jnp.concatenate([jnp.zeros_like(flux[:1]), flux[:-1]], axis=0)
    return flux - lower


def xdiff(field):
    padded = jnp.pad(field, ((0, 0), (0, 0), (1, 1)))
    return padded[:, :, 2:] + padded[:, :, :-2] - 2.0 * field


def mesh_index(line):
    rows = lax.axis_size("px")
    cols = lax.axis_size("py")
    return (line % rows) * cols + line // rows


def ydiff(*fields):
    count = lax.axis_size(LINES)
    up = [(mesh_index(i), mesh_index(i + 1)) for i in range(count - 1)]
    down = [(b, a) for a, b in up]
    depth = fields[0].shape[0]
    below = lax.ppermute(jnp.concatenate([f[:, -1:] for f in fields]), ("px", "py"), up)
    above = lax.ppermute(jnp.concatenate([f[:, :1] for f in fields]), ("px", "py"), down)
    diffs = []
    for k, field in enumerate(fields):
        edge = slice(k * depth, (k + 1) * depth)
        padded = jnp.concatenate([below[edge], field, above[edge]], axis=1)
        diffs.append(padded[:, 2:] + padded[:, :-2] - 2.0 * field)
    return diffs


def along_x(field, matrix, transpose):
    dims = (((2,), (0,)), ((), ())) if transpose else (((2,), (1,)), ((), ()))
    return lax.dot_general(field, matrix, dims, precision=HIGH)


def along_y(matrix, field, transpose):
    dims = (((0,), (0,)), ((), ())) if transpose else (((1,), (0,)), ((), ()))
    return lax.dot_general(matrix, field, dims, precision=HIGH)


def block_to_x(*fields):
    joined = jnp.concatenate(fields, axis=2)
    lines = lax.all_to_all(joined, "px", split_axis=1, concat_axis=0, tiled=True)
    depth = fields[0].shape[2]
    return [jnp.transpose(lines[:, :, k * depth:(k + 1) * depth], (2, 1, 0)) for k in range(len(fields))]


def x_to_block(*fields):
    joined = jnp.concatenate([jnp.transpose(f, (2, 1, 0)) for f in fields], axis=2)
    block = lax.all_to_all(joined, "px", split_axis=0, concat_axis=1, tiled=True)
    depth = fields[0].shape[0]
    return [block[:, :, k * depth:(k + 1) * depth] for k in range(len(fields))]


def x_to_y(*fields):
    joined = jnp.concatenate(fields, axis=2)
    lines = lax.all_to_all(joined, LINES, split_axis=0, concat_axis=0, tiled=True)
    lines = lines.reshape(-1, lines.shape[2])
    width = fields[0].shape[2]
    return [lines[:, k * width:(k + 1) * width] for k in range(len(fields))]


def y_to_x(*fields):
    joined = jnp.concatenate(fields, axis=1)
    count = lax.axis_size(LINES)
    joined = joined.reshape(count, -1, joined.shape[1])
    lines = lax.all_to_all(joined, LINES, split_axis=0, concat_axis=0, tiled=True)
    width = fields[0].shape[1]
    return [lines[:, :, k * width:(k + 1) * width] for k in range(len(fields))]


def block_planes(field):
    count = lax.axis_size(LINES)
    planes = jnp.transpose(field, (2, 1, 0))
    return planes.reshape(count, -1, field.shape[0] * field.shape[1] * field.shape[2] // count // 8)


def planes_to_y(pieces, block):
    rows = lax.axis_size("px")
    cols = lax.axis_size("py")
    depth, width = block[0], block[1]
    tiles = pieces.reshape(cols, rows, width, depth)
    return jnp.transpose(tiles, (0, 2, 1, 3)).reshape(cols * width, rows * depth)


def rows(field):
    return with_layout_constraint(field, Layout(tuple(range(field.ndim))))


def local(initial, conduct, cotangent, inv_x, inv_y):
    (tp,) = x_to_y(block_planes(cotangent))
    ty = planes_to_y(tp, (initial.shape[0], initial.shape[1]))
    lam_second1_y = along_y(inv_y, ty, True)
    first0 = initial + RATE * (ydiff_block(initial) + zoperate_block(initial, conduct))
    f0x, cx = block_to_x(first0, conduct)
    half0 = along_x(f0x, inv_x, False)
    second0 = half0 + RATE * (xdiff(half0) + zoperate(half0, cx))
    count = lax.axis_size(LINES)
    s0y, ls1 = x_to_y(second0, lam_second1_y.reshape(count, -1, lam_second1_y.shape[1]))
    ls1 = rows(ls1.reshape(second0.shape))
    state1_y = rows(along_y(inv_y, s0y, False))
    lam_half1 = ls1 + RATE * (xdiff(ls1) + zoperate(ls1, cx))
    lam_first1 = along_x(lam_half1, inv_x, True)
    (dy_lam_first1,) = ydiff(lam_first1)
    lam_state1 = lam_first1 + RATE * (dy_lam_first1 + zoperate(lam_first1, cx))
    lsy, state1 = x_to_y(rows(lam_state1), state1_y.reshape(lam_state1.shape))
    state1 = rows(state1.reshape(lam_state1.shape))
    (dy_state1,) = ydiff(state1)
    first1 = state1 + RATE * (dy_state1 + zoperate(state1, cx))
    half1 = along_x(first1, inv_x, False)
    grad = -RATE * zstep(ls1) * zstep(half1)
    grad = grad - RATE * zstep(lam_first1) * zstep(state1)
    lam_second0_y = rows(along_y(inv_y, lsy, True))
    (ls0,) = y_to_x(lam_second0_y)
    ls0 = rows(ls0)
    grad = grad - RATE * zstep(ls0) * zstep(half0)
    lam_half0 = ls0 + RATE * (xdiff(ls0) + zoperate(ls0, cx))
    lam_first0 = along_x(lam_half0, inv_x, True)
    lf0, gb = x_to_block(lam_first0, grad)
    gradient = gb - RATE * zstep_block(lf0) * zstep_block(initial)
    adjoint = lf0 + RATE * (ydiff_block(lf0) + zoperate_block(lf0, conduct))
    return (adjoint, gradient)


def solution(mesh):
    in_specs = (P("px", "py", None), P("px", "py", None), P("px", "py", None), P(), P())
    out_specs = (P("px", "py", None), P("px", "py", None))
    return jax.shard_map(local, mesh=mesh, in_specs=in_specs, out_specs=out_specs, check_vma=False)
```

```python
import jax
import jax.numpy as jnp
from jax import lax
from jax.experimental.layout import Layout, with_layout_constraint
from jax.sharding import PartitionSpec as P

RATE = 0.2
LINES = ("py", "px")
HIGH = lax.Precision.HIGH


def ydiff_block(field):
    count = lax.axis_size("py")
    below = lax.ppermute(field[:, -1:], "py", [(i, i + 1) for i in range(count - 1)])
    above = lax.ppermute(field[:, :1], "py", [(i + 1, i) for i in range(count - 1)])
    padded = jnp.concatenate([below, field, above], axis=1)
    return padded[:, 2:] + padded[:, :-2] - 2.0 * field


def zoperate_block(field, conduct):
    upper = jnp.concatenate([field[:, :, 1:], jnp.zeros_like(field[:, :, :1])], axis=2)
    flux = conduct * (upper - field)
    lower = jnp.concatenate([jnp.zeros_like(flux[:, :, :1]), flux[:, :, :-1]], axis=2)
    return flux - lower


def zstep_block(field):
    upper = jnp.concatenate([field[:, :, 1:], jnp.zeros_like(field[:, :, :1])], axis=2)
    return upper - field


def zstep(field):
    upper = jnp.concatenate([field[1:], jnp.zeros_like(field[:1])], axis=0)
    return upper - field


def zoperate(field, conduct):
    flux = conduct * zstep(field)
    lower = jnp.concatenate([jnp.zeros_like(flux[:1]), flux[:-1]], axis=0)
    return flux - lower


def xdiff(field):
    padded = jnp.pad(field, ((0, 0), (0, 0), (1, 1)))
    return padded[:, :, 2:] + padded[:, :, :-2] - 2.0 * field


def mesh_index(line):
    rows = lax.axis_size("px")
    cols = lax.axis_size("py")
    return (line % rows) * cols + line // rows


def ydiff(*fields):
    count = lax.axis_size(LINES)
    up = [(mesh_index(i), mesh_index(i + 1)) for i in range(count - 1)]
    down = [(b, a) for a, b in up]
    depth = fields[0].shape[0]
    below = lax.ppermute(jnp.concatenate([f[:, -1:] for f in fields]), ("px", "py"), up)
    above = lax.ppermute(jnp.concatenate([f[:, :1] for f in fields]), ("px", "py"), down)
    diffs = []
    for k, field in enumerate(fields):
        edge = slice(k * depth, (k + 1) * depth)
        padded = jnp.concatenate([below[edge], field, above[edge]], axis=1)
        diffs.append(padded[:, 2:] + padded[:, :-2] - 2.0 * field)
    return diffs


def along_x(field, matrix, transpose):
    dims = (((2,), (0,)), ((), ())) if transpose else (((2,), (1,)), ((), ()))
    return lax.dot_general(field, matrix, dims, precision=HIGH)


def along_y(matrix, field, transpose):
    dims = (((0,), (0,)), ((), ())) if transpose else (((1,), (0,)), ((), ()))
    return lax.dot_general(matrix, field, dims, precision=HIGH)


def block_to_x(*fields):
    joined = jnp.concatenate(fields, axis=2)
    lines = lax.all_to_all(joined, "px", split_axis=1, concat_axis=0, tiled=True)
    depth = fields[0].shape[2]
    return [jnp.transpose(lines[:, :, k * depth:(k + 1) * depth], (2, 1, 0)) for k in range(len(fields))]


def x_to_block(*fields):
    joined = jnp.concatenate([jnp.transpose(f, (2, 1, 0)) for f in fields], axis=2)
    block = lax.all_to_all(joined, "px", split_axis=0, concat_axis=1, tiled=True)
    depth = fields[0].shape[0]
    return [block[:, :, k * depth:(k + 1) * depth] for k in range(len(fields))]


def x_to_y(*fields):
    joined = jnp.concatenate(fields, axis=2)
    lines = lax.all_to_all(joined, LINES, split_axis=0, concat_axis=0, tiled=True)
    lines = lines.reshape(-1, lines.shape[2])
    width = fields[0].shape[2]
    return [lines[:, k * width:(k + 1) * width] for k in range(len(fields))]


def y_to_x(*fields):
    joined = jnp.concatenate(fields, axis=1)
    count = lax.axis_size(LINES)
    joined = joined.reshape(count, -1, joined.shape[1])
    lines = lax.all_to_all(joined, LINES, split_axis=0, concat_axis=0, tiled=True)
    width = fields[0].shape[1]
    return [lines[:, :, k * width:(k + 1) * width] for k in range(len(fields))]


def block_planes(field):
    count = lax.axis_size(LINES)
    planes = jnp.transpose(field, (2, 1, 0))
    return planes.reshape(count, -1, field.shape[0] * field.shape[1] * field.shape[2] // count // 8)


def planes_to_y(pieces, block):
    rows = lax.axis_size("px")
    cols = lax.axis_size("py")
    depth, width = block[0], block[1]
    tiles = pieces.reshape(cols, rows, width, depth)
    return jnp.transpose(tiles, (0, 2, 1, 3)).reshape(cols * width, rows * depth)


def rows(field):
    return with_layout_constraint(field, Layout(tuple(range(field.ndim))))


def local(initial, conduct, cotangent, inv_x, inv_y):
    (tp,) = x_to_y(block_planes(cotangent))
    ty = planes_to_y(tp, (initial.shape[0], initial.shape[1]))
    lam_second1_y = along_y(inv_y, ty, True)
    first0 = initial + RATE * (ydiff_block(initial) + zoperate_block(initial, conduct))
    f0x, cx = block_to_x(first0, conduct)
    half0 = along_x(f0x, inv_x, False)
    second0 = half0 + RATE * (xdiff(half0) + zoperate(half0, cx))
    count = lax.axis_size(LINES)
    s0y, ls1 = x_to_y(second0, lam_second1_y.reshape(count, -1, lam_second1_y.shape[1]))
    ls1 = rows(ls1.reshape(second0.shape))
    state1_y = rows(along_y(inv_y, s0y, False))
    lam_half1 = ls1 + RATE * (xdiff(ls1) + zoperate(ls1, cx))
    lam_first1 = along_x(lam_half1, inv_x, True)
    (dy_lam_first1,) = ydiff(lam_first1)
    lam_state1 = lam_first1 + RATE * (dy_lam_first1 + zoperate(lam_first1, cx))
    lsy, state1 = x_to_y(rows(lam_state1), state1_y.reshape(lam_state1.shape))
    state1 = rows(state1.reshape(lam_state1.shape))
    (dy_state1,) = ydiff(state1)
    first1 = state1 + RATE * (dy_state1 + zoperate(state1, cx))
    half1 = along_x(first1, inv_x, False)
    grad = -RATE * zstep(ls1) * zstep(half1)
    grad = grad - RATE * zstep(lam_first1) * zstep(state1)
    lam_second0_y = rows(along_y(inv_y, lsy, True))
    (ls0,) = y_to_x(lam_second0_y)
    grad = grad - RATE * zstep(ls0) * zstep(half0)
    lam_half0 = ls0 + RATE * (xdiff(ls0) + zoperate(ls0, cx))
    lam_first0 = along_x(lam_half0, inv_x, True)
    lf0, gb = x_to_block(lam_first0, grad)
    gradient = gb - RATE * zstep_block(lf0) * zstep_block(initial)
    adjoint = lf0 + RATE * (ydiff_block(lf0) + zoperate_block(lf0, conduct))
    return (adjoint, gradient)


def solution(mesh):
    in_specs = (P("px", "py", None), P("px", "py", None), P("px", "py", None), P(), P())
    out_specs = (P("px", "py", None), P("px", "py", None))
    return jax.shard_map(local, mesh=mesh, in_specs=in_specs, out_specs=out_specs, check_vma=False)
```

```python
import jax
import jax.numpy as jnp
from jax import lax
from jax.experimental.layout import Layout, with_layout_constraint
from jax.sharding import PartitionSpec as P

RATE = 0.2
LINES = ("py", "px")
HIGH = lax.Precision.HIGH


def ydiff_block(field):
    count = lax.axis_size("py")
    below = lax.ppermute(field[:, -1:], "py", [(i, i + 1) for i in range(count - 1)])
    above = lax.ppermute(field[:, :1], "py", [(i + 1, i) for i in range(count - 1)])
    padded = jnp.concatenate([below, field, above], axis=1)
    return padded[:, 2:] + padded[:, :-2] - 2.0 * field


def zoperate_block(field, conduct):
    upper = jnp.concatenate([field[:, :, 1:], jnp.zeros_like(field[:, :, :1])], axis=2)
    flux = conduct * (upper - field)
    lower = jnp.concatenate([jnp.zeros_like(flux[:, :, :1]), flux[:, :, :-1]], axis=2)
    return flux - lower


def zstep_block(field):
    upper = jnp.concatenate([field[:, :, 1:], jnp.zeros_like(field[:, :, :1])], axis=2)
    return upper - field


def zstep(field):
    upper = jnp.concatenate([field[1:], jnp.zeros_like(field[:1])], axis=0)
    return upper - field


def zoperate(field, conduct):
    flux = conduct * zstep(field)
    lower = jnp.concatenate([jnp.zeros_like(flux[:1]), flux[:-1]], axis=0)
    return flux - lower


def xdiff(field):
    padded = jnp.pad(field, ((0, 0), (0, 0), (1, 1)))
    return padded[:, :, 2:] + padded[:, :, :-2] - 2.0 * field


def mesh_index(line):
    rows = lax.axis_size("px")
    cols = lax.axis_size("py")
    return (line % rows) * cols + line // rows


def ydiff(*fields):
    count = lax.axis_size(LINES)
    up = [(mesh_index(i), mesh_index(i + 1)) for i in range(count - 1)]
    down = [(b, a) for a, b in up]
    depth = fields[0].shape[0]
    below = lax.ppermute(jnp.concatenate([f[:, -1:] for f in fields]), ("px", "py"), up)
    above = lax.ppermute(jnp.concatenate([f[:, :1] for f in fields]), ("px", "py"), down)
    diffs = []
    for k, field in enumerate(fields):
        edge = slice(k * depth, (k + 1) * depth)
        padded = jnp.concatenate([below[edge], field, above[edge]], axis=1)
        diffs.append(padded[:, 2:] + padded[:, :-2] - 2.0 * field)
    return diffs


def along_x(field, matrix, transpose):
    dims = (((2,), (0,)), ((), ())) if transpose else (((2,), (1,)), ((), ()))
    return lax.dot_general(field, matrix, dims, precision=HIGH)


def along_y(matrix, field, transpose):
    dims = (((0,), (0,)), ((), ())) if transpose else (((1,), (0,)), ((), ()))
    return lax.dot_general(matrix, field, dims, precision=HIGH)


def block_to_x(*fields):
    joined = jnp.concatenate(fields, axis=2)
    lines = lax.all_to_all(joined, "px", split_axis=1, concat_axis=0, tiled=True)
    depth = fields[0].shape[2]
    return [jnp.transpose(lines[:, :, k * depth:(k + 1) * depth], (2, 1, 0)) for k in range(len(fields))]


def x_to_block(*fields):
    joined = jnp.concatenate([jnp.transpose(f, (2, 1, 0)) for f in fields], axis=2)
    block = lax.all_to_all(joined, "px", split_axis=0, concat_axis=1, tiled=True)
    depth = fields[0].shape[0]
    return [block[:, :, k * depth:(k + 1) * depth] for k in range(len(fields))]


def x_to_y(*fields):
    joined = jnp.concatenate(fields, axis=2)
    lines = lax.all_to_all(joined, LINES, split_axis=0, concat_axis=0, tiled=True)
    lines = lines.reshape(-1, lines.shape[2])
    width = fields[0].shape[2]
    return [lines[:, k * width:(k + 1) * width] for k in range(len(fields))]


def y_to_x(*fields):
    joined = jnp.concatenate(fields, axis=1)
    count = lax.axis_size(LINES)
    joined = joined.reshape(count, -1, joined.shape[1])
    lines = lax.all_to_all(joined, LINES, split_axis=0, concat_axis=0, tiled=True)
    width = fields[0].shape[1]
    return [lines[:, :, k * width:(k + 1) * width] for k in range(len(fields))]


def block_planes(field):
    count = lax.axis_size(LINES)
    planes = jnp.transpose(field, (2, 1, 0))
    return planes.reshape(count, -1, field.shape[0] * field.shape[1] * field.shape[2] // count // 8)


def planes_to_y(pieces, block):
    rows = lax.axis_size("px")
    cols = lax.axis_size("py")
    depth, width = block[0], block[1]
    tiles = pieces.reshape(cols, rows, width, depth)
    return jnp.transpose(tiles, (0, 2, 1, 3)).reshape(cols * width, rows * depth)


def rows(field):
    return with_layout_constraint(field, Layout(tuple(range(field.ndim))))


def local(initial, conduct, cotangent, inv_x, inv_y):
    (tp,) = x_to_y(block_planes(cotangent))
    ty = planes_to_y(tp, (initial.shape[0], initial.shape[1]))
    lam_second1_y = along_y(inv_y, ty, True)
    first0 = initial + RATE * (ydiff_block(initial) + zoperate_block(initial, conduct))
    f0x, cx = [rows(v) for v in block_to_x(first0, conduct)]
    half0 = along_x(f0x, inv_x, False)
    second0 = half0 + RATE * (xdiff(half0) + zoperate(half0, cx))
    count = lax.axis_size(LINES)
    s0y, ls1 = x_to_y(second0, lam_second1_y.reshape(count, -1, lam_second1_y.shape[1]))
    ls1 = rows(ls1.reshape(second0.shape))
    state1_y = rows(along_y(inv_y, s0y, False))
    lam_half1 = ls1 + RATE * (xdiff(ls1) + zoperate(ls1, cx))
    lam_first1 = along_x(lam_half1, inv_x, True)
    (dy_lam_first1,) = ydiff(lam_first1)
    lam_state1 = lam_first1 + RATE * (dy_lam_first1 + zoperate(lam_first1, cx))
    lsy, state1 = x_to_y(rows(lam_state1), state1_y.reshape(lam_state1.shape))
    state1 = rows(state1.reshape(lam_state1.shape))
    (dy_state1,) = ydiff(state1)
    first1 = state1 + RATE * (dy_state1 + zoperate(state1, cx))
    half1 = along_x(first1, inv_x, False)
    grad = -RATE * zstep(ls1) * zstep(half1)
    grad = grad - RATE * zstep(lam_first1) * zstep(state1)
    lam_second0_y = rows(along_y(inv_y, lsy, True))
    (ls0,) = y_to_x(lam_second0_y)
    ls0 = rows(ls0)
    grad = grad - RATE * zstep(ls0) * zstep(half0)
    lam_half0 = ls0 + RATE * (xdiff(ls0) + zoperate(ls0, cx))
    lam_first0 = along_x(lam_half0, inv_x, True)
    lf0, gb = x_to_block(lam_first0, grad)
    gradient = gb - RATE * zstep_block(lf0) * zstep_block(initial)
    adjoint = lf0 + RATE * (ydiff_block(lf0) + zoperate_block(lf0, conduct))
    return (adjoint, gradient)


def solution(mesh):
    in_specs = (P("px", "py", None), P("px", "py", None), P("px", "py", None), P(), P())
    out_specs = (P("px", "py", None), P("px", "py", None))
    return jax.shard_map(local, mesh=mesh, in_specs=in_specs, out_specs=out_specs, check_vma=False)
```

```python
import jax
import jax.numpy as jnp
from jax import lax
from jax.experimental.layout import Layout, with_layout_constraint
from jax.sharding import PartitionSpec as P

RATE = 0.2
LINES = ("py", "px")
HIGH = lax.Precision.HIGH


def ydiff_block(field):
    count = lax.axis_size("py")
    below = lax.ppermute(field[:, -1:], "py", [(i, i + 1) for i in range(count - 1)])
    above = lax.ppermute(field[:, :1], "py", [(i + 1, i) for i in range(count - 1)])
    padded = jnp.concatenate([below, field, above], axis=1)
    return padded[:, 2:] + padded[:, :-2] - 2.0 * field


def zoperate_block(field, conduct):
    upper = jnp.concatenate([field[:, :, 1:], jnp.zeros_like(field[:, :, :1])], axis=2)
    flux = conduct * (upper - field)
    lower = jnp.concatenate([jnp.zeros_like(flux[:, :, :1]), flux[:, :, :-1]], axis=2)
    return flux - lower


def zstep_block(field):
    upper = jnp.concatenate([field[:, :, 1:], jnp.zeros_like(field[:, :, :1])], axis=2)
    return upper - field


def zstep(field):
    upper = jnp.concatenate([field[1:], jnp.zeros_like(field[:1])], axis=0)
    return upper - field


def zoperate(field, conduct):
    flux = conduct * zstep(field)
    lower = jnp.concatenate([jnp.zeros_like(flux[:1]), flux[:-1]], axis=0)
    return flux - lower


def xdiff(field):
    padded = jnp.pad(field, ((0, 0), (0, 0), (1, 1)))
    return padded[:, :, 2:] + padded[:, :, :-2] - 2.0 * field


def mesh_index(line):
    rows = lax.axis_size("px")
    cols = lax.axis_size("py")
    return (line % rows) * cols + line // rows


def ydiff(*fields):
    count = lax.axis_size(LINES)
    up = [(mesh_index(i), mesh_index(i + 1)) for i in range(count - 1)]
    down = [(b, a) for a, b in up]
    depth = fields[0].shape[0]
    below = lax.ppermute(jnp.concatenate([f[:, -1:] for f in fields]), ("px", "py"), up)
    above = lax.ppermute(jnp.concatenate([f[:, :1] for f in fields]), ("px", "py"), down)
    diffs = []
    for k, field in enumerate(fields):
        edge = slice(k * depth, (k + 1) * depth)
        padded = jnp.concatenate([below[edge], field, above[edge]], axis=1)
        diffs.append(padded[:, 2:] + padded[:, :-2] - 2.0 * field)
    return diffs


def along_x(field, matrix, transpose):
    dims = (((2,), (0,)), ((), ())) if transpose else (((2,), (1,)), ((), ()))
    return lax.dot_general(field, matrix, dims, precision=HIGH)


def along_y(matrix, field, transpose):
    dims = (((0,), (0,)), ((), ())) if transpose else (((1,), (0,)), ((), ()))
    return lax.dot_general(matrix, field, dims, precision=HIGH)


def block_to_x(*fields):
    joined = jnp.concatenate(fields, axis=2)
    lines = lax.all_to_all(joined, "px", split_axis=1, concat_axis=0, tiled=True)
    depth = fields[0].shape[2]
    return [jnp.transpose(lines[:, :, k * depth:(k + 1) * depth], (2, 1, 0)) for k in range(len(fields))]


def x_to_block(*fields):
    joined = jnp.concatenate([jnp.transpose(f, (2, 1, 0)) for f in fields], axis=2)
    block = lax.all_to_all(joined, "px", split_axis=0, concat_axis=1, tiled=True)
    depth = fields[0].shape[0]
    return [block[:, :, k * depth:(k + 1) * depth] for k in range(len(fields))]


def x_to_y(*fields):
    joined = jnp.concatenate(fields, axis=2)
    lines = lax.all_to_all(joined, LINES, split_axis=0, concat_axis=0, tiled=True)
    lines = lines.reshape(-1, lines.shape[2])
    width = fields[0].shape[2]
    return [lines[:, k * width:(k + 1) * width] for k in range(len(fields))]


def y_to_x(*fields):
    joined = jnp.concatenate(fields, axis=1)
    count = lax.axis_size(LINES)
    joined = joined.reshape(count, -1, joined.shape[1])
    lines = lax.all_to_all(joined, LINES, split_axis=0, concat_axis=0, tiled=True)
    width = fields[0].shape[1]
    return [lines[:, :, k * width:(k + 1) * width] for k in range(len(fields))]


def block_planes(field):
    count = lax.axis_size(LINES)
    planes = jnp.transpose(field, (2, 0, 1))
    return planes.reshape(count, -1, field.shape[0] * field.shape[1] * field.shape[2] // count // 8)


def planes_to_y(pieces, block):
    rows = lax.axis_size("px")
    cols = lax.axis_size("py")
    depth, width = block[0], block[1]
    tiles = pieces.reshape(cols, rows, depth, width)
    return jnp.transpose(tiles, (0, 3, 1, 2)).reshape(cols * width, rows * depth)


def rows(field):
    return with_layout_constraint(field, Layout(tuple(range(field.ndim))))


def local(initial, conduct, cotangent, inv_x, inv_y):
    (tp,) = x_to_y(block_planes(cotangent))
    ty = planes_to_y(tp, (initial.shape[0], initial.shape[1]))
    lam_second1_y = along_y(inv_y, ty, True)
    first0 = initial + RATE * (ydiff_block(initial) + zoperate_block(initial, conduct))
    f0x, cx = block_to_x(first0, conduct)
    half0 = along_x(f0x, inv_x, False)
    second0 = half0 + RATE * (xdiff(half0) + zoperate(half0, cx))
    count = lax.axis_size(LINES)
    s0y, ls1 = x_to_y(second0, lam_second1_y.reshape(count, -1, lam_second1_y.shape[1]))
    ls1 = rows(ls1.reshape(second0.shape))
    state1_y = rows(along_y(inv_y, s0y, False))
    lam_half1 = ls1 + RATE * (xdiff(ls1) + zoperate(ls1, cx))
    lam_first1 = along_x(lam_half1, inv_x, True)
    (dy_lam_first1,) = ydiff(lam_first1)
    lam_state1 = lam_first1 + RATE * (dy_lam_first1 + zoperate(lam_first1, cx))
    lsy, state1 = x_to_y(rows(lam_state1), state1_y.reshape(lam_state1.shape))
    state1 = rows(state1.reshape(lam_state1.shape))
    (dy_state1,) = ydiff(state1)
    first1 = state1 + RATE * (dy_state1 + zoperate(state1, cx))
    half1 = along_x(first1, inv_x, False)
    grad = -RATE * zstep(ls1) * zstep(half1)
    grad = grad - RATE * zstep(lam_first1) * zstep(state1)
    lam_second0_y = rows(along_y(inv_y, lsy, True))
    (ls0,) = y_to_x(lam_second0_y)
    ls0 = rows(ls0)
    grad = grad - RATE * zstep(ls0) * zstep(half0)
    lam_half0 = ls0 + RATE * (xdiff(ls0) + zoperate(ls0, cx))
    lam_first0 = along_x(lam_half0, inv_x, True)
    lf0, gb = x_to_block(lam_first0, grad)
    gradient = gb - RATE * zstep_block(lf0) * zstep_block(initial)
    adjoint = lf0 + RATE * (ydiff_block(lf0) + zoperate_block(lf0, conduct))
    return (adjoint, gradient)


def solution(mesh):
    in_specs = (P("px", "py", None), P("px", "py", None), P("px", "py", None), P(), P())
    out_specs = (P("px", "py", None), P("px", "py", None))
    return jax.shard_map(local, mesh=mesh, in_specs=in_specs, out_specs=out_specs, check_vma=False)
```

```python
import jax
import jax.numpy as jnp
from jax import lax
from jax.experimental.layout import Layout, with_layout_constraint
from jax.sharding import PartitionSpec as P

RATE = 0.2
LINES = ("py", "px")
HIGH = lax.Precision.HIGH


def ydiff_block(field):
    count = lax.axis_size("py")
    below = lax.ppermute(field[:, -1:], "py", [(i, i + 1) for i in range(count - 1)])
    above = lax.ppermute(field[:, :1], "py", [(i + 1, i) for i in range(count - 1)])
    padded = jnp.concatenate([below, field, above], axis=1)
    return padded[:, 2:] + padded[:, :-2] - 2.0 * field


def zoperate_block(field, conduct):
    upper = jnp.concatenate([field[:, :, 1:], jnp.zeros_like(field[:, :, :1])], axis=2)
    flux = conduct * (upper - field)
    lower = jnp.concatenate([jnp.zeros_like(flux[:, :, :1]), flux[:, :, :-1]], axis=2)
    return flux - lower


def zstep_block(field):
    upper = jnp.concatenate([field[:, :, 1:], jnp.zeros_like(field[:, :, :1])], axis=2)
    return upper - field


def zstep(field):
    upper = jnp.concatenate([field[1:], jnp.zeros_like(field[:1])], axis=0)
    return upper - field


def zoperate(field, conduct):
    flux = conduct * zstep(field)
    lower = jnp.concatenate([jnp.zeros_like(flux[:1]), flux[:-1]], axis=0)
    return flux - lower


def xdiff(field):
    padded = jnp.pad(field, ((0, 0), (0, 0), (1, 1)))
    return padded[:, :, 2:] + padded[:, :, :-2] - 2.0 * field


def mesh_index(line):
    rows = lax.axis_size("px")
    cols = lax.axis_size("py")
    return (line % rows) * cols + line // rows


def ydiff(*fields):
    count = lax.axis_size(LINES)
    up = [(mesh_index(i), mesh_index(i + 1)) for i in range(count - 1)]
    down = [(b, a) for a, b in up]
    depth = fields[0].shape[0]
    below = lax.ppermute(jnp.concatenate([f[:, -1:] for f in fields]), ("px", "py"), up)
    above = lax.ppermute(jnp.concatenate([f[:, :1] for f in fields]), ("px", "py"), down)
    diffs = []
    for k, field in enumerate(fields):
        edge = slice(k * depth, (k + 1) * depth)
        padded = jnp.concatenate([below[edge], field, above[edge]], axis=1)
        diffs.append(padded[:, 2:] + padded[:, :-2] - 2.0 * field)
    return diffs


def ydiff_early(field, first_row, last_row):
    count = lax.axis_size(LINES)
    up = [(mesh_index(i), mesh_index(i + 1)) for i in range(count - 1)]
    down = [(b, a) for a, b in up]
    below = lax.ppermute(last_row, ("px", "py"), up)
    above = lax.ppermute(first_row, ("px", "py"), down)
    padded = jnp.concatenate([below, field, above], axis=1)
    return padded[:, 2:] + padded[:, :-2] - 2.0 * field


def along_x(field, matrix, transpose):
    dims = (((2,), (0,)), ((), ())) if transpose else (((2,), (1,)), ((), ()))
    return lax.dot_general(field, matrix, dims, precision=HIGH)


def along_y(matrix, field, transpose):
    dims = (((0,), (0,)), ((), ())) if transpose else (((1,), (0,)), ((), ()))
    return lax.dot_general(matrix, field, dims, precision=HIGH)


def block_to_x(*fields):
    joined = jnp.concatenate(fields, axis=2)
    lines = lax.all_to_all(joined, "px", split_axis=1, concat_axis=0, tiled=True)
    depth = fields[0].shape[2]
    return [jnp.transpose(lines[:, :, k * depth:(k + 1) * depth], (2, 1, 0)) for k in range(len(fields))]


def x_to_block(*fields):
    joined = jnp.concatenate([jnp.transpose(f, (2, 1, 0)) for f in fields], axis=2)
    block = lax.all_to_all(joined, "px", split_axis=0, concat_axis=1, tiled=True)
    depth = fields[0].shape[0]
    return [block[:, :, k * depth:(k + 1) * depth] for k in range(len(fields))]


def x_to_y(*fields):
    joined = jnp.concatenate(fields, axis=2)
    lines = lax.all_to_all(joined, LINES, split_axis=0, concat_axis=0, tiled=True)
    lines = lines.reshape(-1, lines.shape[2])
    width = fields[0].shape[2]
    return [lines[:, k * width:(k + 1) * width] for k in range(len(fields))]


def y_to_x(*fields):
    joined = jnp.concatenate(fields, axis=1)
    count = lax.axis_size(LINES)
    joined = joined.reshape(count, -1, joined.shape[1])
    lines = lax.all_to_all(joined, LINES, split_axis=0, concat_axis=0, tiled=True)
    width = fields[0].shape[1]
    return [lines[:, :, k * width:(k + 1) * width] for k in range(len(fields))]


def block_planes(field):
    count = lax.axis_size(LINES)
    planes = jnp.transpose(field, (2, 0, 1))
    return planes.reshape(count, -1, field.shape[0] * field.shape[1] * field.shape[2] // count // 8)


def planes_to_y(pieces, block):
    rows = lax.axis_size("px")
    cols = lax.axis_size("py")
    depth, width = block[0], block[1]
    tiles = pieces.reshape(cols, rows, depth, width)
    return jnp.transpose(tiles, (0, 3, 1, 2)).reshape(cols * width, rows * depth)


def rows(field):
    return with_layout_constraint(field, Layout(tuple(range(field.ndim))))


def local(initial, conduct, cotangent, inv_x, inv_y):
    (tp,) = x_to_y(block_planes(cotangent))
    ty = planes_to_y(tp, (initial.shape[0], initial.shape[1]))
    lam_second1_y = along_y(inv_y, ty, True)
    first0 = initial + RATE * (ydiff_block(initial) + zoperate_block(initial, conduct))
    f0x, cx = block_to_x(first0, conduct)
    half0 = along_x(f0x, inv_x, False)
    second0 = half0 + RATE * (xdiff(half0) + zoperate(half0, cx))
    count = lax.axis_size(LINES)
    s0y, ls1 = x_to_y(second0, lam_second1_y.reshape(count, -1, lam_second1_y.shape[1]))
    ls1 = rows(ls1.reshape(second0.shape))
    state1_y = rows(along_y(inv_y, s0y, False))
    lam_half1 = ls1 + RATE * (xdiff(ls1) + zoperate(ls1, cx))
    lam_first1 = along_x(lam_half1, inv_x, True)
    dy_lam_first1 = ydiff_early(
        lam_first1,
        along_x(lam_half1[:, :1], inv_x, True),
        along_x(lam_half1[:, -1:], inv_x, True),
    )
    lam_state1 = lam_first1 + RATE * (dy_lam_first1 + zoperate(lam_first1, cx))
    lsy, state1 = x_to_y(rows(lam_state1), state1_y.reshape(lam_state1.shape))
    state1 = rows(state1.reshape(lam_state1.shape))
    (dy_state1,) = ydiff(state1)
    first1 = state1 + RATE * (dy_state1 + zoperate(state1, cx))
    half1 = along_x(first1, inv_x, False)
    grad = -RATE * zstep(ls1) * zstep(half1)
    grad = grad - RATE * zstep(lam_first1) * zstep(state1)
    lam_second0_y = rows(along_y(inv_y, lsy, True))
    (ls0,) = y_to_x(lam_second0_y)
    ls0 = rows(ls0)
    grad = grad - RATE * zstep(ls0) * zstep(half0)
    lam_half0 = ls0 + RATE * (xdiff(ls0) + zoperate(ls0, cx))
    lam_first0 = along_x(lam_half0, inv_x, True)
    lf0, gb = x_to_block(lam_first0, grad)
    gradient = gb - RATE * zstep_block(lf0) * zstep_block(initial)
    adjoint = lf0 + RATE * (ydiff_block(lf0) + zoperate_block(lf0, conduct))
    return (adjoint, gradient)


def solution(mesh):
    in_specs = (P("px", "py", None), P("px", "py", None), P("px", "py", None), P(), P())
    out_specs = (P("px", "py", None), P("px", "py", None))
    return jax.shard_map(local, mesh=mesh, in_specs=in_specs, out_specs=out_specs, check_vma=False)
```

```python
import jax
import jax.numpy as jnp
from jax import lax
from jax.experimental.layout import Layout, with_layout_constraint
from jax.sharding import PartitionSpec as P

RATE = 0.2
LINES = ("py", "px")
HIGH = lax.Precision.HIGH


def ydiff_block(field):
    count = lax.axis_size("py")
    below = lax.ppermute(field[:, -1:], "py", [(i, i + 1) for i in range(count - 1)])
    above = lax.ppermute(field[:, :1], "py", [(i + 1, i) for i in range(count - 1)])
    padded = jnp.concatenate([below, field, above], axis=1)
    return padded[:, 2:] + padded[:, :-2] - 2.0 * field


def zoperate_block(field, conduct):
    upper = jnp.concatenate([field[:, :, 1:], jnp.zeros_like(field[:, :, :1])], axis=2)
    flux = conduct * (upper - field)
    lower = jnp.concatenate([jnp.zeros_like(flux[:, :, :1]), flux[:, :, :-1]], axis=2)
    return flux - lower


def zstep_block(field):
    upper = jnp.concatenate([field[:, :, 1:], jnp.zeros_like(field[:, :, :1])], axis=2)
    return upper - field


def zstep(field):
    upper = jnp.concatenate([field[1:], jnp.zeros_like(field[:1])], axis=0)
    return upper - field


def zoperate(field, conduct):
    flux = conduct * zstep(field)
    lower = jnp.concatenate([jnp.zeros_like(flux[:1]), flux[:-1]], axis=0)
    return flux - lower


def xdiff(field):
    padded = jnp.pad(field, ((0, 0), (0, 0), (1, 1)))
    return padded[:, :, 2:] + padded[:, :, :-2] - 2.0 * field


def mesh_index(line):
    rows = lax.axis_size("px")
    cols = lax.axis_size("py")
    return (line % rows) * cols + line // rows


def ydiff(*fields):
    count = lax.axis_size(LINES)
    up = [(mesh_index(i), mesh_index(i + 1)) for i in range(count - 1)]
    down = [(b, a) for a, b in up]
    depth = fields[0].shape[0]
    below = lax.ppermute(jnp.concatenate([f[:, -1:] for f in fields]), ("px", "py"), up)
    above = lax.ppermute(jnp.concatenate([f[:, :1] for f in fields]), ("px", "py"), down)
    diffs = []
    for k, field in enumerate(fields):
        edge = slice(k * depth, (k + 1) * depth)
        padded = jnp.concatenate([below[edge], field, above[edge]], axis=1)
        diffs.append(padded[:, 2:] + padded[:, :-2] - 2.0 * field)
    return diffs


def along_x(field, matrix, transpose):
    dims = (((2,), (0,)), ((), ())) if transpose else (((2,), (1,)), ((), ()))
    return lax.dot_general(field, matrix, dims, precision=HIGH)


def along_y(matrix, field, transpose):
    dims = (((0,), (0,)), ((), ())) if transpose else (((1,), (0,)), ((), ()))
    return lax.dot_general(matrix, field, dims, precision=HIGH)


def block_to_x(*fields):
    joined = jnp.concatenate(fields, axis=2)
    lines = lax.all_to_all(joined, "px", split_axis=1, concat_axis=0, tiled=True)
    depth = fields[0].shape[2]
    return [jnp.transpose(lines[:, :, k * depth:(k + 1) * depth], (2, 1, 0)) for k in range(len(fields))]


def x_to_block(*fields):
    joined = jnp.transpose(jnp.concatenate(fields, axis=0), (2, 1, 0))
    block = lax.all_to_all(joined, "px", split_axis=0, concat_axis=1, tiled=True)
    depth = fields[0].shape[0]
    return [block[:, :, k * depth:(k + 1) * depth] for k in range(len(fields))]


def x_to_y(*fields):
    joined = jnp.concatenate(fields, axis=2)
    lines = lax.all_to_all(joined, LINES, split_axis=0, concat_axis=0, tiled=True)
    lines = lines.reshape(-1, lines.shape[2])
    width = fields[0].shape[2]
    return [lines[:, k * width:(k + 1) * width] for k in range(len(fields))]


def y_to_x(*fields):
    joined = jnp.concatenate(fields, axis=1)
    count = lax.axis_size(LINES)
    joined = joined.reshape(count, -1, joined.shape[1])
    lines = lax.all_to_all(joined, LINES, split_axis=0, concat_axis=0, tiled=True)
    width = fields[0].shape[1]
    return [lines[:, :, k * width:(k + 1) * width] for k in range(len(fields))]


def block_planes(field):
    count = lax.axis_size(LINES)
    planes = jnp.transpose(field, (2, 0, 1))
    return planes.reshape(count, -1, field.shape[0] * field.shape[1] * field.shape[2] // count // 8)


def planes_to_y(pieces, block):
    rows = lax.axis_size("px")
    cols = lax.axis_size("py")
    depth, width = block[0], block[1]
    tiles = pieces.reshape(cols, rows, depth, width)
    return jnp.transpose(tiles, (0, 3, 1, 2)).reshape(cols * width, rows * depth)


def rows(field):
    return with_layout_constraint(field, Layout(tuple(range(field.ndim))))


def local(initial, conduct, cotangent, inv_x, inv_y):
    (tp,) = x_to_y(block_planes(cotangent))
    ty = planes_to_y(tp, (initial.shape[0], initial.shape[1]))
    lam_second1_y = along_y(inv_y, ty, True)
    first0 = initial + RATE * (ydiff_block(initial) + zoperate_block(initial, conduct))
    f0x, cx = block_to_x(first0, conduct)
    half0 = along_x(f0x, inv_x, False)
    second0 = half0 + RATE * (xdiff(half0) + zoperate(half0, cx))
    count = lax.axis_size(LINES)
    s0y, ls1 = x_to_y(second0, lam_second1_y.reshape(count, -1, lam_second1_y.shape[1]))
    ls1 = rows(ls1.reshape(second0.shape))
    state1_y = rows(along_y(inv_y, s0y, False))
    lam_half1 = ls1 + RATE * (xdiff(ls1) + zoperate(ls1, cx))
    lam_first1 = along_x(lam_half1, inv_x, True)
    (dy_lam_first1,) = ydiff(lam_first1)
    lam_state1 = lam_first1 + RATE * (dy_lam_first1 + zoperate(lam_first1, cx))
    lsy, state1 = x_to_y(rows(lam_state1), state1_y.reshape(lam_state1.shape))
    state1 = rows(state1.reshape(lam_state1.shape))
    (dy_state1,) = ydiff(state1)
    first1 = state1 + RATE * (dy_state1 + zoperate(state1, cx))
    half1 = along_x(first1, inv_x, False)
    grad = -RATE * zstep(ls1) * zstep(half1)
    grad = grad - RATE * zstep(lam_first1) * zstep(state1)
    lam_second0_y = rows(along_y(inv_y, lsy, True))
    (ls0,) = y_to_x(lam_second0_y)
    ls0 = rows(ls0)
    grad = grad - RATE * zstep(ls0) * zstep(half0)
    lam_half0 = ls0 + RATE * (xdiff(ls0) + zoperate(ls0, cx))
    lam_first0 = along_x(lam_half0, inv_x, True)
    lf0, gb = x_to_block(lam_first0, grad)
    gradient = gb - RATE * zstep_block(lf0) * zstep_block(initial)
    adjoint = lf0 + RATE * (ydiff_block(lf0) + zoperate_block(lf0, conduct))
    return (adjoint, gradient)


def solution(mesh):
    in_specs = (P("px", "py", None), P("px", "py", None), P("px", "py", None), P(), P())
    out_specs = (P("px", "py", None), P("px", "py", None))
    return jax.shard_map(local, mesh=mesh, in_specs=in_specs, out_specs=out_specs, check_vma=False)
```

```python
import jax
import jax.numpy as jnp
from jax import lax
from jax.experimental.layout import Layout, with_layout_constraint
from jax.sharding import PartitionSpec as P

RATE = 0.2
LINES = ("py", "px")
HIGH = lax.Precision.HIGH


def ydiff_block(field):
    count = lax.axis_size("py")
    below = lax.ppermute(field[:, -1:], "py", [(i, i + 1) for i in range(count - 1)])
    above = lax.ppermute(field[:, :1], "py", [(i + 1, i) for i in range(count - 1)])
    padded = jnp.concatenate([below, field, above], axis=1)
    return padded[:, 2:] + padded[:, :-2] - 2.0 * field


def zoperate_block(field, conduct):
    upper = jnp.concatenate([field[:, :, 1:], jnp.zeros_like(field[:, :, :1])], axis=2)
    flux = conduct * (upper - field)
    lower = jnp.concatenate([jnp.zeros_like(flux[:, :, :1]), flux[:, :, :-1]], axis=2)
    return flux - lower


def zstep_block(field):
    upper = jnp.concatenate([field[:, :, 1:], jnp.zeros_like(field[:, :, :1])], axis=2)
    return upper - field


def zstep(field):
    upper = jnp.concatenate([field[1:], jnp.zeros_like(field[:1])], axis=0)
    return upper - field


def zoperate(field, conduct):
    flux = conduct * zstep(field)
    lower = jnp.concatenate([jnp.zeros_like(flux[:1]), flux[:-1]], axis=0)
    return flux - lower


def xdiff(field):
    padded = jnp.pad(field, ((0, 0), (0, 0), (1, 1)))
    return padded[:, :, 2:] + padded[:, :, :-2] - 2.0 * field


def mesh_index(line):
    rows = lax.axis_size("px")
    cols = lax.axis_size("py")
    return (line % rows) * cols + line // rows


def ydiff(*fields):
    count = lax.axis_size(LINES)
    up = [(mesh_index(i), mesh_index(i + 1)) for i in range(count - 1)]
    down = [(b, a) for a, b in up]
    depth = fields[0].shape[0]
    below = lax.ppermute(jnp.concatenate([f[:, -1:] for f in fields]), ("px", "py"), up)
    above = lax.ppermute(jnp.concatenate([f[:, :1] for f in fields]), ("px", "py"), down)
    diffs = []
    for k, field in enumerate(fields):
        edge = slice(k * depth, (k + 1) * depth)
        padded = jnp.concatenate([below[edge], field, above[edge]], axis=1)
        diffs.append(padded[:, 2:] + padded[:, :-2] - 2.0 * field)
    return diffs


def along_x(field, matrix, transpose):
    dims = (((2,), (0,)), ((), ())) if transpose else (((2,), (1,)), ((), ()))
    return lax.dot_general(field, matrix, dims, precision=HIGH)


def along_y(matrix, field, transpose):
    dims = (((0,), (0,)), ((), ())) if transpose else (((1,), (0,)), ((), ()))
    return lax.dot_general(matrix, field, dims, precision=HIGH)


def block_to_x(*fields):
    joined = jnp.concatenate(fields, axis=2)
    lines = lax.all_to_all(joined, "px", split_axis=1, concat_axis=0, tiled=True)
    depth = fields[0].shape[2]
    return [jnp.transpose(lines[:, :, k * depth:(k + 1) * depth], (2, 1, 0)) for k in range(len(fields))]


def x_to_block(*fields):
    joined = jnp.concatenate([jnp.transpose(f, (2, 1, 0)) for f in fields], axis=2)
    block = lax.all_to_all(joined, "px", split_axis=0, concat_axis=1, tiled=True)
    depth = fields[0].shape[0]
    return [block[:, :, k * depth:(k + 1) * depth] for k in range(len(fields))]


def x_to_y(*fields):
    joined = jnp.concatenate(fields, axis=2)
    lines = lax.all_to_all(joined, LINES, split_axis=0, concat_axis=0, tiled=True)
    lines = lines.reshape(-1, lines.shape[2])
    width = fields[0].shape[2]
    return [lines[:, k * width:(k + 1) * width] for k in range(len(fields))]


def y_to_x(*fields):
    joined = jnp.concatenate(fields, axis=1)
    count = lax.axis_size(LINES)
    joined = joined.reshape(count, -1, joined.shape[1])
    lines = lax.all_to_all(joined, LINES, split_axis=0, concat_axis=0, tiled=True)
    width = fields[0].shape[1]
    return [lines[:, :, k * width:(k + 1) * width] for k in range(len(fields))]


def block_planes(field):
    count = lax.axis_size(LINES)
    planes = jnp.transpose(field, (2, 0, 1))
    return planes.reshape(count, -1, field.shape[0] * field.shape[1] * field.shape[2] // count // 8)


def planes_to_y(pieces, block):
    rows = lax.axis_size("px")
    cols = lax.axis_size("py")
    depth, width = block[0], block[1]
    tiles = pieces.reshape(cols, rows, depth, width)
    return jnp.transpose(tiles, (0, 3, 1, 2)).reshape(cols * width, rows * depth)


def rows(field):
    return with_layout_constraint(field, Layout(tuple(range(field.ndim))))


def local(initial, conduct, cotangent, inv_x, inv_y):
    (tp,) = x_to_y(block_planes(cotangent))
    ty = planes_to_y(tp, (initial.shape[0], initial.shape[1]))
    lam_second1_y = along_y(inv_y, ty, True)
    first0 = initial + RATE * (ydiff_block(initial) + zoperate_block(initial, conduct))
    f0x, cx = block_to_x(first0, conduct)
    half0 = along_x(f0x, inv_x, False)
    second0 = half0 + RATE * (xdiff(half0) + zoperate(half0, cx))
    count = lax.axis_size(LINES)
    s0y, ls1 = x_to_y(second0, lam_second1_y.reshape(count, -1, lam_second1_y.shape[1]))
    ls1 = ls1.reshape(second0.shape)
    state1_y = rows(along_y(inv_y, s0y, False))
    lam_half1 = ls1 + RATE * (xdiff(ls1) + zoperate(ls1, cx))
    lam_first1 = along_x(lam_half1, inv_x, True)
    (dy_lam_first1,) = ydiff(lam_first1)
    lam_state1 = lam_first1 + RATE * (dy_lam_first1 + zoperate(lam_first1, cx))
    lsy, state1 = x_to_y(rows(lam_state1), state1_y.reshape(lam_state1.shape))
    state1 = rows(state1.reshape(lam_state1.shape))
    (dy_state1,) = ydiff(state1)
    first1 = state1 + RATE * (dy_state1 + zoperate(state1, cx))
    half1 = along_x(first1, inv_x, False)
    grad = -RATE * zstep(ls1) * zstep(half1)
    grad = grad - RATE * zstep(lam_first1) * zstep(state1)
    lam_second0_y = rows(along_y(inv_y, lsy, True))
    (ls0,) = y_to_x(lam_second0_y)
    ls0 = rows(ls0)
    grad = grad - RATE * zstep(ls0) * zstep(half0)
    lam_half0 = ls0 + RATE * (xdiff(ls0) + zoperate(ls0, cx))
    lam_first0 = along_x(lam_half0, inv_x, True)
    lf0, gb = x_to_block(lam_first0, grad)
    gradient = gb - RATE * zstep_block(lf0) * zstep_block(initial)
    adjoint = lf0 + RATE * (ydiff_block(lf0) + zoperate_block(lf0, conduct))
    return (adjoint, gradient)


def solution(mesh):
    in_specs = (P("px", "py", None), P("px", "py", None), P("px", "py", None), P(), P())
    out_specs = (P("px", "py", None), P("px", "py", None))
    return jax.shard_map(local, mesh=mesh, in_specs=in_specs, out_specs=out_specs, check_vma=False)
```

```python
import jax
import jax.numpy as jnp
from jax import lax
from jax.experimental.layout import Layout, with_layout_constraint
from jax.sharding import PartitionSpec as P

RATE = 0.2
LINES = ("py", "px")
HIGH = lax.Precision.HIGH


def ydiff_block(field):
    count = lax.axis_size("py")
    below = lax.ppermute(field[:, -1:], "py", [(i, i + 1) for i in range(count - 1)])
    above = lax.ppermute(field[:, :1], "py", [(i + 1, i) for i in range(count - 1)])
    padded = jnp.concatenate([below, field, above], axis=1)
    return padded[:, 2:] + padded[:, :-2] - 2.0 * field


def zoperate_block(field, conduct):
    upper = jnp.concatenate([field[:, :, 1:], jnp.zeros_like(field[:, :, :1])], axis=2)
    flux = conduct * (upper - field)
    lower = jnp.concatenate([jnp.zeros_like(flux[:, :, :1]), flux[:, :, :-1]], axis=2)
    return flux - lower


def zstep_block(field):
    upper = jnp.concatenate([field[:, :, 1:], jnp.zeros_like(field[:, :, :1])], axis=2)
    return upper - field


def zstep(field):
    upper = jnp.concatenate([field[1:], jnp.zeros_like(field[:1])], axis=0)
    return upper - field


def zoperate(field, conduct):
    flux = conduct * zstep(field)
    lower = jnp.concatenate([jnp.zeros_like(flux[:1]), flux[:-1]], axis=0)
    return flux - lower


def xdiff(field):
    padded = jnp.pad(field, ((0, 0), (0, 0), (1, 1)))
    return padded[:, :, 2:] + padded[:, :, :-2] - 2.0 * field


def mesh_index(line):
    rows = lax.axis_size("px")
    cols = lax.axis_size("py")
    return (line % rows) * cols + line // rows


def ydiff(*fields):
    count = lax.axis_size(LINES)
    up = [(mesh_index(i), mesh_index(i + 1)) for i in range(count - 1)]
    down = [(b, a) for a, b in up]
    depth = fields[0].shape[0]
    below = lax.ppermute(jnp.concatenate([f[:, -1:] for f in fields]), ("px", "py"), up)
    above = lax.ppermute(jnp.concatenate([f[:, :1] for f in fields]), ("px", "py"), down)
    diffs = []
    for k, field in enumerate(fields):
        edge = slice(k * depth, (k + 1) * depth)
        padded = jnp.concatenate([below[edge], field, above[edge]], axis=1)
        diffs.append(padded[:, 2:] + padded[:, :-2] - 2.0 * field)
    return diffs


def along_x(field, matrix, transpose):
    dims = (((2,), (0,)), ((), ())) if transpose else (((2,), (1,)), ((), ()))
    return lax.dot_general(field, matrix, dims, precision=HIGH)


def along_y(matrix, field, transpose):
    dims = (((0,), (0,)), ((), ())) if transpose else (((1,), (0,)), ((), ()))
    return lax.dot_general(matrix, field, dims, precision=HIGH)


def block_to_x(*fields):
    joined = jnp.concatenate(fields, axis=2)
    lines = lax.all_to_all(joined, "px", split_axis=1, concat_axis=0, tiled=True)
    depth = fields[0].shape[2]
    return [jnp.transpose(lines[:, :, k * depth:(k + 1) * depth], (2, 1, 0)) for k in range(len(fields))]


def x_to_block(*fields):
    joined = jnp.concatenate([jnp.transpose(f, (2, 1, 0)) for f in fields], axis=2)
    block = lax.all_to_all(joined, "px", split_axis=0, concat_axis=1, tiled=True)
    depth = fields[0].shape[0]
    return [block[:, :, k * depth:(k + 1) * depth] for k in range(len(fields))]


def x_to_y(*fields):
    joined = jnp.concatenate(fields, axis=2)
    lines = lax.all_to_all(joined, LINES, split_axis=0, concat_axis=0, tiled=True)
    lines = lines.reshape(-1, lines.shape[2])
    width = fields[0].shape[2]
    return [lines[:, k * width:(k + 1) * width] for k in range(len(fields))]


def y_to_x(*fields):
    joined = jnp.concatenate(fields, axis=1)
    count = lax.axis_size(LINES)
    joined = joined.reshape(count, -1, joined.shape[1])
    lines = lax.all_to_all(joined, LINES, split_axis=0, concat_axis=0, tiled=True)
    width = fields[0].shape[1]
    return [lines[:, :, k * width:(k + 1) * width] for k in range(len(fields))]


def block_planes(field):
    count = lax.axis_size(LINES)
    planes = jnp.transpose(field, (2, 0, 1))
    return planes.reshape(count, -1, field.shape[0] * field.shape[1] * field.shape[2] // count // 8)


def planes_to_y(pieces, block):
    rows = lax.axis_size("px")
    cols = lax.axis_size("py")
    depth, width = block[0], block[1]
    tiles = pieces.reshape(cols, rows, depth, width)
    return jnp.transpose(tiles, (0, 3, 1, 2)).reshape(cols * width, rows * depth)


def rows(field):
    return with_layout_constraint(field, Layout(tuple(range(field.ndim))))


def local(initial, conduct, cotangent, inv_x, inv_y):
    (tp,) = x_to_y(block_planes(cotangent))
    ty = planes_to_y(tp, (initial.shape[0], initial.shape[1]))
    lam_second1_y = along_y(inv_y, ty, True)
    first0 = initial + RATE * (ydiff_block(initial) + zoperate_block(initial, conduct))
    f0x, cx = block_to_x(first0, conduct)
    half0 = along_x(f0x, inv_x, False)
    second0 = half0 + RATE * (xdiff(half0) + zoperate(half0, cx))
    count = lax.axis_size(LINES)
    s0y, ls1 = x_to_y(second0, lam_second1_y.reshape(count, -1, lam_second1_y.shape[1]))
    ls1 = ls1.reshape(second0.shape)
    state1_y = rows(along_y(inv_y, s0y, False))
    lam_half1 = ls1 + RATE * (xdiff(ls1) + zoperate(ls1, cx))
    lam_first1 = along_x(lam_half1, inv_x, True)
    (dy_lam_first1,) = ydiff(lam_first1)
    lam_state1 = lam_first1 + RATE * (dy_lam_first1 + zoperate(lam_first1, cx))
    lsy, state1 = x_to_y(rows(lam_state1), state1_y.reshape(lam_state1.shape))
    state1 = state1.reshape(lam_state1.shape)
    (dy_state1,) = ydiff(state1)
    first1 = state1 + RATE * (dy_state1 + zoperate(state1, cx))
    half1 = along_x(first1, inv_x, False)
    grad = -RATE * zstep(ls1) * zstep(half1)
    grad = grad - RATE * zstep(lam_first1) * zstep(state1)
    lam_second0_y = rows(along_y(inv_y, lsy, True))
    (ls0,) = y_to_x(lam_second0_y)
    ls0 = rows(ls0)
    grad = grad - RATE * zstep(ls0) * zstep(half0)
    lam_half0 = ls0 + RATE * (xdiff(ls0) + zoperate(ls0, cx))
    lam_first0 = along_x(lam_half0, inv_x, True)
    lf0, gb = x_to_block(lam_first0, grad)
    gradient = gb - RATE * zstep_block(lf0) * zstep_block(initial)
    adjoint = lf0 + RATE * (ydiff_block(lf0) + zoperate_block(lf0, conduct))
    return (adjoint, gradient)


def solution(mesh):
    in_specs = (P("px", "py", None), P("px", "py", None), P("px", "py", None), P(), P())
    out_specs = (P("px", "py", None), P("px", "py", None))
    return jax.shard_map(local, mesh=mesh, in_specs=in_specs, out_specs=out_specs, check_vma=False)
```

```python
import jax
import jax.numpy as jnp
from jax import lax
from jax.experimental.layout import Layout, with_layout_constraint
from jax.sharding import PartitionSpec as P

RATE = 0.2
LINES = ("py", "px")
HIGH = lax.Precision.HIGH


def ydiff_block(field):
    count = lax.axis_size("py")
    below = lax.ppermute(field[:, -1:], "py", [(i, i + 1) for i in range(count - 1)])
    above = lax.ppermute(field[:, :1], "py", [(i + 1, i) for i in range(count - 1)])
    padded = jnp.concatenate([below, field, above], axis=1)
    return padded[:, 2:] + padded[:, :-2] - 2.0 * field


def zoperate_block(field, conduct):
    upper = jnp.concatenate([field[:, :, 1:], jnp.zeros_like(field[:, :, :1])], axis=2)
    flux = conduct * (upper - field)
    lower = jnp.concatenate([jnp.zeros_like(flux[:, :, :1]), flux[:, :, :-1]], axis=2)
    return flux - lower


def zstep_block(field):
    upper = jnp.concatenate([field[:, :, 1:], jnp.zeros_like(field[:, :, :1])], axis=2)
    return upper - field


def zstep(field):
    upper = jnp.concatenate([field[1:], jnp.zeros_like(field[:1])], axis=0)
    return upper - field


def zoperate(field, conduct):
    flux = conduct * zstep(field)
    lower = jnp.concatenate([jnp.zeros_like(flux[:1]), flux[:-1]], axis=0)
    return flux - lower


def xdiff(field):
    padded = jnp.pad(field, ((0, 0), (0, 0), (1, 1)))
    return padded[:, :, 2:] + padded[:, :, :-2] - 2.0 * field


def mesh_index(line):
    rows = lax.axis_size("px")
    cols = lax.axis_size("py")
    return (line % rows) * cols + line // rows


def ydiff(*fields):
    count = lax.axis_size(LINES)
    up = [(mesh_index(i), mesh_index(i + 1)) for i in range(count - 1)]
    down = [(b, a) for a, b in up]
    depth = fields[0].shape[0]
    below = lax.ppermute(jnp.concatenate([f[:, -1:] for f in fields]), ("px", "py"), up)
    above = lax.ppermute(jnp.concatenate([f[:, :1] for f in fields]), ("px", "py"), down)
    diffs = []
    for k, field in enumerate(fields):
        edge = slice(k * depth, (k + 1) * depth)
        padded = jnp.concatenate([below[edge], field, above[edge]], axis=1)
        diffs.append(padded[:, 2:] + padded[:, :-2] - 2.0 * field)
    return diffs


def along_x(field, matrix, transpose):
    dims = (((2,), (0,)), ((), ())) if transpose else (((2,), (1,)), ((), ()))
    return lax.dot_general(field, matrix, dims, precision=HIGH)


def along_y(matrix, field, transpose):
    dims = (((0,), (0,)), ((), ())) if transpose else (((1,), (0,)), ((), ()))
    return lax.dot_general(matrix, field, dims, precision=HIGH)


def block_to_x(*fields):
    joined = jnp.concatenate(fields, axis=2)
    lines = lax.all_to_all(joined, "px", split_axis=1, concat_axis=0, tiled=True)
    depth = fields[0].shape[2]
    return [jnp.transpose(lines[:, :, k * depth:(k + 1) * depth], (2, 1, 0)) for k in range(len(fields))]


def x_to_block(*fields):
    joined = jnp.concatenate([jnp.transpose(f, (2, 1, 0)) for f in fields], axis=2)
    block = lax.all_to_all(joined, "px", split_axis=0, concat_axis=1, tiled=True)
    depth = fields[0].shape[0]
    return [block[:, :, k * depth:(k + 1) * depth] for k in range(len(fields))]


def x_to_y(*fields):
    joined = jnp.concatenate(fields, axis=2)
    lines = lax.all_to_all(joined, LINES, split_axis=0, concat_axis=0, tiled=True)
    lines = lines.reshape(-1, lines.shape[2])
    width = fields[0].shape[2]
    return [lines[:, k * width:(k + 1) * width] for k in range(len(fields))]


def y_to_x(*fields):
    joined = jnp.concatenate(fields, axis=1)
    count = lax.axis_size(LINES)
    joined = joined.reshape(count, -1, joined.shape[1])
    lines = lax.all_to_all(joined, LINES, split_axis=0, concat_axis=0, tiled=True)
    width = fields[0].shape[1]
    return [lines[:, :, k * width:(k + 1) * width] for k in range(len(fields))]


def block_planes(field):
    count = lax.axis_size(LINES)
    planes = jnp.transpose(field, (2, 0, 1))
    return planes.reshape(count, -1, field.shape[0] * field.shape[1] * field.shape[2] // count // 8)


def planes_to_y(pieces, block):
    rows = lax.axis_size("px")
    cols = lax.axis_size("py")
    depth, width = block[0], block[1]
    tiles = pieces.reshape(cols, rows, depth, width)
    return jnp.transpose(tiles, (0, 3, 1, 2)).reshape(cols * width, rows * depth)


def rows(field):
    return with_layout_constraint(field, Layout(tuple(range(field.ndim))))


def local(initial, conduct, cotangent, inv_x, inv_y):
    (tp,) = x_to_y(block_planes(cotangent))
    ty = planes_to_y(tp, (initial.shape[0], initial.shape[1]))
    lam_second1_y = along_y(inv_y, ty, True)
    first0 = initial + RATE * (ydiff_block(initial) + zoperate_block(initial, conduct))
    f0x, cx = block_to_x(first0, conduct)
    half0 = along_x(f0x, inv_x, False)
    second0 = half0 + RATE * (xdiff(half0) + zoperate(half0, cx))
    count = lax.axis_size(LINES)
    s0y, ls1 = x_to_y(second0, lam_second1_y.reshape(count, -1, lam_second1_y.shape[1]))
    ls1 = ls1.reshape(second0.shape)
    state1_y = rows(along_y(inv_y, s0y, False))
    lam_half1 = ls1 + RATE * (xdiff(ls1) + zoperate(ls1, cx))
    lam_first1 = along_x(lam_half1, inv_x, True)
    (dy_lam_first1,) = ydiff(lam_first1)
    lam_state1 = lam_first1 + RATE * (dy_lam_first1 + zoperate(lam_first1, cx))
    lsy, state1 = x_to_y(lam_state1, state1_y.reshape(lam_state1.shape))
    state1 = rows(state1.reshape(lam_state1.shape))
    (dy_state1,) = ydiff(state1)
    first1 = state1 + RATE * (dy_state1 + zoperate(state1, cx))
    half1 = along_x(first1, inv_x, False)
    grad = -RATE * zstep(ls1) * zstep(half1)
    grad = grad - RATE * zstep(lam_first1) * zstep(state1)
    lam_second0_y = rows(along_y(inv_y, lsy, True))
    (ls0,) = y_to_x(lam_second0_y)
    ls0 = rows(ls0)
    grad = grad - RATE * zstep(ls0) * zstep(half0)
    lam_half0 = ls0 + RATE * (xdiff(ls0) + zoperate(ls0, cx))
    lam_first0 = along_x(lam_half0, inv_x, True)
    lf0, gb = x_to_block(lam_first0, grad)
    gradient = gb - RATE * zstep_block(lf0) * zstep_block(initial)
    adjoint = lf0 + RATE * (ydiff_block(lf0) + zoperate_block(lf0, conduct))
    return (adjoint, gradient)


def solution(mesh):
    in_specs = (P("px", "py", None), P("px", "py", None), P("px", "py", None), P(), P())
    out_specs = (P("px", "py", None), P("px", "py", None))
    return jax.shard_map(local, mesh=mesh, in_specs=in_specs, out_specs=out_specs, check_vma=False)
```
